512 devices in a mesh: segment: 8 (over z), owner: 64 (over y, x, core).
Axes of the slice: x: 4, y: 8, z: 8, core: 2. Of those that a mesh axis runs over, the one named last changes fastest.
Arguments:
- layer_input_rows: bfloat16 [8, 8192, 4096], P('segment', 'owner'), may hold values from -6 to 6
- output_gradient: bfloat16 [8, 8192, 1024], P('segment', 'owner'), may hold values from -6 to 6
- tenant: int32 [8192, 1], P('owner'), may hold values from 0 to 63; in each aligned block of 128 rows (0 to 127, 128 to 255, ...) at most 4 rows name the same one
- adapter_owner_index: int32 [64], replicated, may hold values from 0 to 63, each once
- adapter_down_weight: bfloat16 [8, 64, 4096, 64], P('segment', 'owner'), may hold values from -0.09375 to 0.09375
- adapter_up_weight: bfloat16 [8, 64, 64, 1024], P('segment', 'owner'), may hold values from -0.1875 to 0.1875
Outputs:
- passed_grad: bfloat16 [8, 8192, 4096], P('segment', 'owner')
- grad_down: float32 [8, 64, 4096, 64], P('segment', 'owner')
- grad_up: float32 [8, 64, 64, 1024], P('segment', 'owner')
The draws below stay inside these ranges and needn't reach their ends.
Inputs may be any that keep to these rules, and one draw needn't show every extreme that they name: `tenant`: within the rows of one device no adapter is named by more than 4 rows, and in every draw some device names some adapter exactly 4 times. `adapter_owner_index`: each owner index appears once.
All inputs are finite; a program needn't handle non-finite values.
Results may differ from the reference program's by a relative error of at most 0.014.
Values may be sent and summed in bfloat16 or wider, within the bound.
No kernel may reach another device: no remote copies, remote signals or barrier semaphores. Data moves between devices by JAX's collectives and lax.ppermute only.
A program may use at most 128 MiB of HBM per device.

```python
import math
import jax
import jax.numpy as jnp
import numpy as np
from jax import lax

MODEL_WIDTH = 4096
VALUE_WIDTH = 1024
ADAPTER_RANK = 64
TOK_DEV = 128
ROW_LIMIT = 4
ADAPTERS = 64
TOKENS = 8192
N_SEGMENT = 8
N_OWNER = 64


def block_scale(key, shape, shards, least, top_value):
    loudness, own = 1.0, jax.random.fold_in(key, 6)
    for position, parts in shards:
        heights = jnp.exp(jax.random.uniform(jax.random.fold_in(own, position), (parts,), jnp.float32, least / len(shards), top_value / len(shards)))
        loudness = loudness * jnp.repeat(heights, shape[position] // parts).reshape([-1 if axis == position else 1 for axis in range(len(shape))])
    return loudness


def deal_out(stream_key, own, number, rows, amount, top, reach, skew):
    order = jax.random.permutation(stream_key, amount)
    heavy_load, common = portions_of(amount, rows * top, reach, skew, True), portions_of(amount, rows * top, reach, skew, False)
    places = jnp.arange(amount)

    def named(sizes, turn):
        used = int((sizes > 0).sum())
        fixed = max(1, used // 4)
        shifted = fixed + (places - fixed + turn * (used - fixed)) % max(1, amount - fixed)
        return jnp.zeros((amount,), jnp.int32).at[order[jnp.where(places < fixed, places, shifted)]].set(jnp.asarray(sizes, jnp.int32))

    sizes = jnp.where(number % 4 == 0, named(heavy_load, number // 4), named(common, number - number // 4 - 1))
    mixed = jax.random.permutation(jax.random.fold_in(own, 3), amount)
    source_of, sink = mixed[0:amount // 2 * 2:2], mixed[1:amount // 2 * 2:2]
    slack = jnp.minimum(sizes[source_of] - 1, reach - sizes[sink]) // 2
    slack = jnp.where((source_of == order[0]) | (sink == order[0]) | (sizes[sink] == 0), 0, jnp.maximum(slack, 0))
    shifted = jax.random.randint(jax.random.fold_in(own, 4), (amount // 2,), 0, 1 << 20) % (slack + 1)
    sizes = sizes.at[source_of].add(-shifted).at[sink].add(shifted)
    members = jnp.searchsorted(jnp.cumsum(sizes), jnp.arange(rows * top), side="right").astype(jnp.int32)
    grid = members.reshape(top, rows).T
    grid = grid[jax.random.permutation(jax.random.fold_in(own, 1), rows)]
    turn = jax.random.randint(jax.random.fold_in(own, 2), (rows, 1), 0, top)
    return jnp.take_along_axis(grid, (jnp.arange(top)[None, :] + turn) % top, axis=1)


def portions_of(amount, total, bound, lean, full):
    portions = [(1 << 20) // math.isqrt(grade ** lean) + 1 for grade in range(1, amount + 1)]
    largest = bound if full else min(bound, max(-(-total // amount), total * portions[0] // sum(portions)))
    least = 1 if total - largest >= amount - 1 else 0
    given, surplus = [largest] + [least] * (amount - 1), total - largest - least * (amount - 1)
    while surplus > 0:
        candidates = [i for i in range(1, amount) if given[i] < largest] or [i for i in range(1, amount) if given[i] < bound]
        pool, remaining = sum([portions[i] for i in candidates]), surplus
        for i in candidates:
            more = min(bound - given[i], max(1, remaining * portions[i] // pool), surplus)
            given[i] = given[i] + more
            surplus = surplus - more
    return np.array(given)


def noise(own_key, dims, width, bound, split=(), kind=jnp.bfloat16):
    entries = jax.random.normal(own_key, dims, jnp.float32) * width
    if len(split) > 0:
        entries = block_scale(own_key, dims, split, -0.22, 0.18) * entries
    return jnp.clip(entries, min=-bound, max=bound).astype(kind)


def setup_inputs(seed: int = 0) -> dict:
    arg_keys = jax.random.split(jax.random.key(seed), 7)
    layer_input_rows = noise(arg_keys[0], (N_SEGMENT, TOKENS, MODEL_WIDTH), 1.0, 6.0, ((0, 8), (1, 64)))
    output_gradient = noise(arg_keys[1], (N_SEGMENT, TOKENS, VALUE_WIDTH), 1.0, 6.0, ((0, 8), (1, 64)))
    tenant_keys = jax.random.split(jax.random.fold_in(arg_keys[2], 1), TOKENS // TOK_DEV)
    tenant_turns = jax.random.permutation(jax.random.fold_in(arg_keys[2], 3), TOKENS // TOK_DEV)
    tenant = jax.vmap(lambda own, number: deal_out(jax.random.fold_in(arg_keys[2], 2), own, number, TOK_DEV, ADAPTERS, 1, ROW_LIMIT, 2))(tenant_keys, tenant_turns).reshape((TOKENS, 1))
    adapter_owner_index = jax.random.permutation(arg_keys[3], ADAPTERS).astype(jnp.int32)
    adapter_down_weight = noise(arg_keys[4], (N_SEGMENT, N_OWNER, MODEL_WIDTH, ADAPTER_RANK), MODEL_WIDTH ** -0.5, 0.09375, ((0, 8), (1, 64)))
    adapter_up_weight = noise(arg_keys[5], (N_SEGMENT, N_OWNER, ADAPTER_RANK, VALUE_WIDTH), VALUE_WIDTH ** -0.5, 0.1875, ((0, 8), (1, 64)))
    return {"layer_input_rows": layer_input_rows, "output_gradient": output_gradient, "tenant": tenant, "adapter_owner_index": adapter_owner_index, "adapter_down_weight": adapter_down_weight, "adapter_up_weight": adapter_up_weight}


adapter_scale = 2.0


def reference(layer_input_rows, output_gradient, tenant, adapter_owner_index, adapter_down_weight, adapter_up_weight):
    ids = tenant[:, 0].astype(jnp.int32)
    dest = adapter_owner_index[ids].astype(jnp.int32)
    source = jnp.arange(TOKENS, dtype=jnp.int32) // TOK_DEV
    onehot = (dest[:, None] == jnp.arange(N_OWNER, dtype=jnp.int32)[None, :]).astype(jnp.int32)
    onehot = onehot.reshape(N_OWNER, TOK_DEV, N_OWNER)
    ranked = (jnp.cumsum(onehot, axis=1) - 1) * onehot
    rank = jnp.sum(ranked, axis=2).reshape(TOKENS).astype(jnp.int32)
    location_mask = dest * (N_OWNER * ROW_LIMIT) + source * ROW_LIMIT + rank
    row_count_total = N_OWNER * N_OWNER * ROW_LIMIT
    highest_precision = lax.Precision.HIGHEST

    def single_section(items):
        inputs, gradient_list, down_factor, up_factor = items
        xbuf = jnp.zeros((row_count_total, MODEL_WIDTH), jnp.float32).at[location_mask].set(inputs.astype(jnp.float32))
        xbuf = xbuf.reshape(N_OWNER, N_OWNER * ROW_LIMIT, MODEL_WIDTH)
        gradient_buffer = jnp.zeros((row_count_total, VALUE_WIDTH), jnp.float32).at[location_mask].set(gradient_list.astype(jnp.float32))
        gradient_buffer = gradient_buffer.reshape(N_OWNER, N_OWNER * ROW_LIMIT, VALUE_WIDTH)
        down32 = down_factor.astype(jnp.float32)
        up_factor_float32 = up_factor.astype(jnp.float32)
        scale_weight = adapter_scale * jnp.einsum('lgd,lwd->lgw', gradient_buffer, up_factor_float32, precision=highest_precision)
        projected_rows = jnp.einsum('ord,odk->ork', xbuf, down32, precision=highest_precision)
        down_gradient = jnp.einsum('ord,ork->odk', xbuf, scale_weight, precision=highest_precision)
        up_gradient = jnp.einsum('gbl,gbw->glw', projected_rows, gradient_buffer, precision=highest_precision)
        term = jnp.einsum('ork,odk->ord', scale_weight, down32, precision=highest_precision).astype(jnp.bfloat16)
        term = term.reshape(row_count_total, MODEL_WIDTH)[location_mask]
        return term, down_gradient, up_gradient

    partial_terms, down_gradient, up_gradient = lax.map(single_section, (layer_input_rows, output_gradient, adapter_down_weight, adapter_up_weight))
    suffix = jnp.flip(jnp.cumsum(jnp.flip(partial_terms.astype(jnp.float32), 0), 0), 0)
    return suffix.astype(jnp.bfloat16), down_gradient, up_gradient
```

```python
import jax
import jax.numpy as jnp
from jax import lax
from jax.experimental import pallas as pl
from jax.experimental.pallas import tpu as pltpu
from jax.sharding import PartitionSpec as P

adapter_scale = 2.0
row_limit = 4
group = 2 * row_limit
f32 = jnp.float32
bf16 = jnp.bfloat16


def dot(a, b, contract):
    return lax.dot_general(a, b, (contract, ((), ())), preferred_element_type=f32)


def iota(shape, axis):
    return lax.broadcasted_iota(jnp.int32, shape, axis)


def half_of(shape):
    return (iota(shape, 0) // row_limit) % 2


def place_gradient_kernel(tenant_ref, owner_ref, grad_ref, placing_ref, send_ref):
    tok_rows = tenant_ref.shape[1]
    owners = owner_ref.shape[1]
    slots = owners * group
    named = (iota((owners, tok_rows), 0) == tenant_ref[...]).astype(bf16)
    held = (iota((owners, owners), 0) == owner_ref[...]).astype(bf16)
    goes = dot(held, named, ((1,), (0,)))
    before = (iota((tok_rows, tok_rows), 0) < iota((tok_rows, tok_rows), 1)).astype(bf16)
    rank = dot(goes.astype(bf16), before, ((1,), (0,)))
    key = (goes * (rank + 1.0)).astype(bf16)
    spread = (iota((slots, owners), 0) // group == iota((slots, owners), 1)).astype(bf16)
    wide_key = dot(spread, key, ((1,), (0,)))
    index = (iota((slots, tok_rows), 0) % row_limit + 1).astype(f32)
    placing = wide_key == index
    placing_ref[...] = placing.astype(bf16)
    half = half_of((slots, tok_rows))
    width = grad_ref.shape[1] // 2
    lower = jnp.where(placing & (half == 0), 1.0, 0.0).astype(bf16)
    upper = jnp.where(placing & (half == 1), 1.0, 0.0).astype(bf16)
    sent = dot(lower, grad_ref[:, :width], ((1,), (0,))) + dot(upper, grad_ref[:, width:], ((1,), (0,)))
    send_ref[...] = sent.astype(bf16).reshape(send_ref.shape)


def place_inputs_kernel(placing_ref, low_ref, high_ref, send_ref):
    placing = placing_ref[...]
    half = half_of(placing.shape)
    zero = jnp.zeros_like(placing)
    lower = jnp.where(half == 0, placing, zero)
    upper = jnp.where(half == 1, placing, zero)
    sent = dot(lower, low_ref[...], ((1,), (0,))) + dot(upper, high_ref[...], ((1,), (0,)))
    send_ref[...] = sent.astype(bf16).reshape(send_ref.shape)


def both_halves(x):
    blocks = x.reshape(x.shape[0] // group, group, x.shape[1])
    return (blocks + pltpu.roll(blocks, row_limit, 1)).reshape(x.shape)


def coef_kernel(grad_ref, up_ref, coef_ref):
    grads = grad_ref[...].reshape(coef_ref.shape[0], grad_ref.shape[2])
    width = grad_ref.shape[2]
    low = dot(grads, up_ref[:, :width], ((1,), (1,)))
    high = dot(grads, up_ref[:, width:], ((1,), (1,)))
    part = jnp.where(half_of(low.shape) == 0, low, high)
    coef_ref[...] = (adapter_scale * both_halves(part)).astype(bf16)


def term_kernel(place_ref, coef_ref, low_ref, high_ref, out_ref):
    place = place_ref[0]
    sections = coef_ref.shape[0]
    parts = []
    for k in range(sections):
        parts.append(jnp.where(place <= k, coef_ref[k], jnp.zeros_like(coef_ref[k])))
    coef = jnp.concatenate(parts, axis=1)
    low = dot(coef, low_ref[...], ((1,), (0,)))
    high = dot(coef, high_ref[...], ((1,), (0,)))
    out = jnp.where(half_of(low.shape) == 0, low, high)
    out_ref[...] = out.astype(bf16).reshape(out_ref.shape)


def weight_gradient_kernel(rows_ref, grads_ref, coef_ref, down_ref, grad_down_ref, grad_up_ref):
    slots = coef_ref.shape[0]
    rank = coef_ref.shape[1]
    width = rows_ref.shape[2]
    out_width = grads_ref.shape[2]
    rows = rows_ref[...].reshape(slots, width)
    grads = grads_ref[...].reshape(slots, out_width)
    half = half_of((slots, rank))
    coef = coef_ref[...]
    zero = jnp.zeros_like(coef)
    pair = jnp.concatenate([jnp.where(half == 0, coef, zero), jnp.where(half == 1, coef, zero)], axis=1)
    down = dot(pair, rows, ((0,), (0,)))
    grad_down_ref[:, :width] = down[:rank]
    grad_down_ref[:, width:] = down[rank:]
    low = dot(rows, down_ref[:, :width], ((1,), (1,)))
    high = dot(rows, down_ref[:, width:], ((1,), (1,)))
    proj = both_halves(jnp.where(half == 0, low, high)).astype(bf16)
    pair = jnp.concatenate([jnp.where(half == 0, proj, zero), jnp.where(half == 1, proj, zero)], axis=1)
    up = dot(pair, grads, ((0,), (0,)))
    grad_up_ref[:, :out_width] = up[:rank]
    grad_up_ref[:, out_width:] = up[rank:]


def unplace_kernel(placing_ref, rows_ref, out_ref):
    placing = placing_ref[...]
    mine = half_of(placing.shape) == pl.program_id(1)
    picked = jnp.where(mine, placing, jnp.zeros_like(placing))
    rows = rows_ref[...].reshape(placing.shape[0], rows_ref.shape[2])
    out_ref[...] = dot(picked, rows, ((0,), (0,))).astype(bf16)


def local(
    layer_input_rows,
    output_gradient,
    tenant,
    adapter_owner_index,
    adapter_down_weight,
    adapter_up_weight,
):
    inputs = layer_input_rows[0]
    gradient_list = output_gradient[0]
    tok_rows, width = inputs.shape
    out_width = gradient_list.shape[1]
    owners = adapter_owner_index.shape[0]
    rank = adapter_up_weight.shape[2]
    slots = owners * group
    sections = lax.axis_size("segment")
    place = lax.axis_index("segment").astype(jnp.int32).reshape(1)
    down_factor = adapter_down_weight[0, 0].T
    up_factor = adapter_up_weight[0, 0]
    half_width = width // 2
    steps = 4
    block = half_width // steps
    shape = jax.ShapeDtypeStruct

    all_down = lax.all_gather(down_factor, "segment").reshape(sections * rank, width)

    placing, send_grads = pl.pallas_call(
        place_gradient_kernel,
        out_shape=(shape((slots, tok_rows), bf16), shape((owners, group, out_width // 2), bf16)),
        name="place_gradient",
    )(tenant.reshape(1, tok_rows), adapter_owner_index.reshape(1, owners), gradient_list)
    recv_grads = lax.all_to_all(send_grads, "owner", split_axis=0, concat_axis=0, tiled=True)

    send_inputs = pl.pallas_call(
        place_inputs_kernel,
        grid=(steps,),
        in_specs=[
            pl.BlockSpec((slots, tok_rows), lambda c: (0, 0)),
            pl.BlockSpec((tok_rows, block), lambda c: (0, c)),
            pl.BlockSpec((tok_rows, block), lambda c: (0, c + steps)),
        ],
        out_specs=pl.BlockSpec((owners, group, block), lambda c: (0, 0, c)),
        out_shape=shape((owners, group, half_width), bf16),
        name="place_inputs",
    )(placing, inputs, inputs)

    coef = pl.pallas_call(
        coef_kernel,
        out_shape=shape((slots, rank), bf16),
        name="coef",
    )(recv_grads, up_factor)

    recv_inputs = lax.all_to_all(send_inputs, "owner", split_axis=0, concat_axis=0, tiled=True)
    all_coef = lax.all_gather(coef, "segment")

    terms = pl.pallas_call(
        term_kernel,
        grid=(steps,),
        in_specs=[
            pl.BlockSpec(memory_space=pltpu.SMEM),
            pl.BlockSpec((sections, slots, rank), lambda c: (0, 0, 0)),
            pl.BlockSpec((sections * rank, block), lambda c: (0, c)),
            pl.BlockSpec((sections * rank, block), lambda c: (0, c + steps)),
        ],
        out_specs=pl.BlockSpec((owners, group, block), lambda c: (0, 0, c)),
        out_shape=shape((owners, group, half_width), bf16),
        name="term",
    )(place, all_coef, all_down, all_down)
    returned = lax.all_to_all(terms, "owner", split_axis=0, concat_axis=0, tiled=True)

    grad_down, grad_up = pl.pallas_call(
        weight_gradient_kernel,
        out_shape=(shape((rank, width), f32), shape((rank, out_width), f32)),
        name="weight_gradient",
    )(recv_inputs, recv_grads, coef, down_factor)

    passed = pl.pallas_call(
        unplace_kernel,
        grid=(steps, 2),
        in_specs=[
            pl.BlockSpec((slots, tok_rows), lambda c, h: (0, 0)),
            pl.BlockSpec((owners, group, block), lambda c, h: (0, 0, c)),
        ],
        out_specs=pl.BlockSpec((tok_rows, block), lambda c, h: (0, h * steps + c)),
        out_shape=shape((tok_rows, width), bf16),
        name="unplace",
    )(placing, returned)

    return (passed[None], grad_down.T[None, None], grad_up[None, None])


def solution(mesh):
    return jax.shard_map(
        local,
        mesh=mesh,
        in_specs=(
            P("segment", "owner", None),
            P("segment", "owner", None),
            P("owner", None),
            P(),
            P("segment", "owner", None, None),
            P("segment", "owner", None, None),
        ),
        out_specs=(
            P("segment", "owner", None),
            P("segment", "owner", None, None),
            P("segment", "owner", None, None),
        ),
        check_vma=False,
    )
```

```python
import jax
import jax.numpy as jnp
from jax import lax
from jax.experimental import pallas as pl
from jax.experimental.pallas import tpu as pltpu
from jax.sharding import PartitionSpec as P

adapter_scale = 2.0
row_limit = 4
group = 2 * row_limit
f32 = jnp.float32
bf16 = jnp.bfloat16


def dot(a, b, contract):
    return lax.dot_general(a, b, (contract, ((), ())), preferred_element_type=f32)


def iota(shape, axis):
    return lax.broadcasted_iota(jnp.int32, shape, axis)


def half_of(shape):
    return (iota(shape, 0) // row_limit) % 2


def place_gradient_kernel(tenant_ref, owner_ref, grad_ref, placing_ref, send_ref):
    tok_rows = tenant_ref.shape[1]
    owners = owner_ref.shape[1]
    slots = owners * group
    named = iota((owners, tok_rows), 0) == tenant_ref[...]
    before = (iota((tok_rows, tok_rows), 0) < iota((tok_rows, tok_rows), 1)).astype(bf16)
    rank = dot(named.astype(bf16), before, ((1,), (0,)))
    key = jnp.where(named, rank + 1.0, 0.0).astype(bf16)
    held = (iota((slots, owners), 0) // group == owner_ref[...]).astype(bf16)
    wide_key = dot(held, key, ((1,), (0,)))
    index = (iota((slots, tok_rows), 0) % row_limit + 1).astype(f32)
    placing = wide_key == index
    placing_ref[...] = placing.astype(bf16)
    half = half_of((slots, tok_rows))
    width = grad_ref.shape[1] // 2
    lower = jnp.where(placing & (half == 0), 1.0, 0.0).astype(bf16)
    upper = jnp.where(placing & (half == 1), 1.0, 0.0).astype(bf16)
    sent = dot(lower, grad_ref[:, :width], ((1,), (0,))) + dot(upper, grad_ref[:, width:], ((1,), (0,)))
    send_ref[...] = sent.astype(bf16).reshape(send_ref.shape)


def place_inputs_kernel(placing_ref, low_ref, high_ref, send_ref, back_ref):
    placing = placing_ref[...]
    half = half_of(placing.shape)
    zero = jnp.zeros_like(placing)
    lower = jnp.where(half == 0, placing, zero)
    upper = jnp.where(half == 1, placing, zero)

    @pl.when(pl.program_id(0) == 0)
    def _():
        back_ref[0] = lower.astype(f32).T.astype(bf16)
        back_ref[1] = upper.astype(f32).T.astype(bf16)

    sent = dot(lower, low_ref[...], ((1,), (0,))) + dot(upper, high_ref[...], ((1,), (0,)))
    send_ref[...] = sent.astype(bf16).reshape(send_ref.shape)


def both_halves(x):
    blocks = x.reshape(x.shape[0] // group, group, x.shape[1])
    return (blocks + pltpu.roll(blocks, row_limit, 1)).reshape(x.shape)


def coef_kernel(grad_ref, up_ref, coef_ref):
    grads = grad_ref[...].reshape(coef_ref.shape[0], grad_ref.shape[2])
    width = grad_ref.shape[2]
    low = dot(grads, up_ref[:, :width], ((1,), (1,)))
    high = dot(grads, up_ref[:, width:], ((1,), (1,)))
    part = jnp.where(half_of(low.shape) == 0, low, high)
    coef_ref[...] = (adapter_scale * both_halves(part)).astype(bf16)


def term_kernel(place_ref, coef_ref, *refs):
    sections = coef_ref.shape[0]
    lows, highs, out_ref = refs[:sections], refs[sections:-1], refs[-1]
    place = place_ref[0]
    parts = []
    for step in range(sections):
        part = coef_ref[(place + step) % sections]
        parts.append(jnp.where(place + step < sections, part, jnp.zeros_like(part)))
    coef = jnp.concatenate(parts, axis=1)
    low = dot(coef, jnp.concatenate([r[...] for r in lows], axis=0), ((1,), (0,)))
    high = dot(coef, jnp.concatenate([r[...] for r in highs], axis=0), ((1,), (0,)))
    out = jnp.where(half_of(low.shape) == 0, low, high)
    out_ref[...] = out.astype(bf16).reshape(out_ref.shape)


def weight_gradient_kernel(rows_ref, grads_ref, coef_ref, down_ref, grad_down_ref, grad_up_ref):
    slots = coef_ref.shape[0]
    rank = coef_ref.shape[1]
    width = rows_ref.shape[2]
    out_width = grads_ref.shape[2]
    rows = rows_ref[...].reshape(slots, width)
    grads = grads_ref[...].reshape(slots, out_width)
    half = half_of((slots, rank))
    coef = coef_ref[...]
    zero = jnp.zeros_like(coef)
    pair = jnp.concatenate([jnp.where(half == 0, coef, zero), jnp.where(half == 1, coef, zero)], axis=1)
    down = dot(pair, rows, ((0,), (0,)))
    grad_down_ref[:, :width] = down[:rank]
    grad_down_ref[:, width:] = down[rank:]
    low = dot(rows, down_ref[:, :width], ((1,), (1,)))
    high = dot(rows, down_ref[:, width:], ((1,), (1,)))
    proj = both_halves(jnp.where(half == 0, low, high)).astype(bf16)
    pair = jnp.concatenate([jnp.where(half == 0, proj, zero), jnp.where(half == 1, proj, zero)], axis=1)
    up = dot(pair, grads, ((0,), (0,)))
    grad_up_ref[:, :out_width] = up[:rank]
    grad_up_ref[:, out_width:] = up[rank:]


def unplace_kernel(back_ref, rows_ref, out_ref):
    rows = rows_ref[...].reshape(back_ref.shape[2], rows_ref.shape[2])
    out_ref[...] = dot(back_ref[0], rows, ((1,), (0,))).astype(bf16)


def ring_round(blocks, axis):
    count = lax.axis_size(axis)
    down = [(i, (i - 1) % count) for i in range(count)]
    up = [(i, (i + 1) % count) for i in range(count)]
    step = (len(blocks) + 1) // 2
    new = dict(blocks)
    new[step] = lax.ppermute(blocks[step - 1], axis, down)
    if step < count - step:
        new[count - step] = lax.ppermute(blocks[(count - step + 1) % count], axis, up)
    return new


def local(
    layer_input_rows,
    output_gradient,
    tenant,
    adapter_owner_index,
    adapter_down_weight,
    adapter_up_weight,
):
    inputs = layer_input_rows[0]
    gradient_list = output_gradient[0]
    tok_rows, width = inputs.shape
    out_width = gradient_list.shape[1]
    owners = adapter_owner_index.shape[0]
    rank = adapter_up_weight.shape[2]
    slots = owners * group
    sections = lax.axis_size("segment")
    place = lax.axis_index("segment").astype(jnp.int32).reshape(1)
    down_factor = adapter_down_weight[0, 0].T
    up_factor = adapter_up_weight[0, 0]
    half_width = width // 2
    steps = 4
    block = half_width // steps
    shape = jax.ShapeDtypeStruct

    placing, send_grads = pl.pallas_call(
        place_gradient_kernel,
        out_shape=(shape((slots, tok_rows), bf16), shape((owners, group, out_width // 2), bf16)),
        name="place_gradient",
    )(tenant.reshape(1, tok_rows), adapter_owner_index.reshape(1, owners), gradient_list)
    send_grads, ring_start = lax.optimization_barrier((send_grads, down_factor))
    recv_grads = lax.all_to_all(send_grads, "owner", split_axis=0, concat_axis=0, tiled=True)

    send_inputs, back = pl.pallas_call(
        place_inputs_kernel,
        grid=(steps,),
        in_specs=[
            pl.BlockSpec((slots, tok_rows), lambda c: (0, 0)),
            pl.BlockSpec((tok_rows, block), lambda c: (0, c)),
            pl.BlockSpec((tok_rows, block), lambda c: (0, c + steps)),
        ],
        out_specs=(
            pl.BlockSpec((owners, group, block), lambda c: (0, 0, c)),
            pl.BlockSpec((2, tok_rows, slots), lambda c: (0, 0, 0)),
        ),
        out_shape=(shape((owners, group, half_width), bf16), shape((2, tok_rows, slots), bf16)),
        name="place_inputs",
    )(placing, inputs, inputs)

    blocks = ring_round({0: ring_start}, "segment")
    send_inputs, blocks = lax.optimization_barrier((send_inputs, blocks))

    coef = pl.pallas_call(
        coef_kernel,
        out_shape=shape((slots, rank), bf16),
        name="coef",
    )(recv_grads, up_factor)

    recv_inputs = lax.all_to_all(send_inputs, "owner", split_axis=0, concat_axis=0, tiled=True)
    all_coef = lax.all_gather(coef, "segment")
    while len(blocks) < sections:
        blocks = ring_round(blocks, "segment")
    downs = [blocks[step] for step in range(sections)]

    terms = pl.pallas_call(
        term_kernel,
        grid=(steps,),
        in_specs=[
            pl.BlockSpec(memory_space=pltpu.SMEM),
            pl.BlockSpec((sections, slots, rank), lambda c: (0, 0, 0)),
        ]
        + [pl.BlockSpec((rank, block), lambda c: (0, c))] * sections
        + [pl.BlockSpec((rank, block), lambda c: (0, c + steps))] * sections,
        out_specs=pl.BlockSpec((owners, group, block), lambda c: (0, 0, c)),
        out_shape=shape((owners, group, half_width), bf16),
        name="term",
    )(place, all_coef, *downs, *downs)
    returned = lax.all_to_all(terms, "owner", split_axis=0, concat_axis=0, tiled=True)

    grad_down, grad_up = pl.pallas_call(
        weight_gradient_kernel,
        out_shape=(shape((rank, width), f32), shape((rank, out_width), f32)),
        name="weight_gradient",
    )(recv_inputs, recv_grads, coef, down_factor)

    back_steps = 2
    back_block = half_width // back_steps
    passed = pl.pallas_call(
        unplace_kernel,
        grid=(back_steps, 2),
        in_specs=[
            pl.BlockSpec((1, tok_rows, slots), lambda c, h: (h, 0, 0)),
            pl.BlockSpec((owners, group, back_block), lambda c, h: (0, 0, c)),
        ],
        out_specs=pl.BlockSpec((tok_rows, back_block), lambda c, h: (0, h * back_steps + c)),
        out_shape=shape((tok_rows, width), bf16),
        name="unplace",
    )(back, returned)

    return (passed[None], grad_down.T[None, None], grad_up[None, None])


def solution(mesh):
    return jax.shard_map(
        local,
        mesh=mesh,
        in_specs=(
            P("segment", "owner", None),
            P("segment", "owner", None),
            P("owner", None),
            P(),
            P("segment", "owner", None, None),
            P("segment", "owner", None, None),
        ),
        out_specs=(
            P("segment", "owner", None),
            P("segment", "owner", None, None),
            P("segment", "owner", None, None),
        ),
        check_vma=False,
    )
```

```python
import jax
import jax.numpy as jnp
from jax import lax
from jax.experimental import pallas as pl
from jax.experimental.pallas import tpu as pltpu
from jax.sharding import PartitionSpec as P

adapter_scale = 2.0
row_limit = 4
group = 2 * row_limit
f32 = jnp.float32
bf16 = jnp.bfloat16


def dot(a, b, contract):
    return lax.dot_general(a, b, (contract, ((), ())), preferred_element_type=f32)


def iota(shape, axis):
    return lax.broadcasted_iota(jnp.int32, shape, axis)


def half_of(shape):
    return (iota(shape, 0) // row_limit) % 2


def place_gradient_kernel(tenant_ref, owner_ref, grad_ref, placing_ref, send_ref):
    tok_rows = tenant_ref.shape[1]
    owners = owner_ref.shape[1]
    slots = owners * group
    named = iota((owners, tok_rows), 0) == tenant_ref[...]
    before = (iota((tok_rows, tok_rows), 0) < iota((tok_rows, tok_rows), 1)).astype(bf16)
    rank = dot(named.astype(bf16), before, ((1,), (0,)))
    key = jnp.where(named, rank + 1.0, 0.0).astype(bf16)
    held = (iota((slots, owners), 0) // group == owner_ref[...]).astype(bf16)
    wide_key = dot(held, key, ((1,), (0,)))
    index = (iota((slots, tok_rows), 0) % row_limit + 1).astype(f32)
    placing = wide_key == index
    placing_ref[...] = placing.astype(bf16)
    half = half_of((slots, tok_rows))
    width = grad_ref.shape[1] // 2
    lower = jnp.where(placing & (half == 0), 1.0, 0.0).astype(bf16)
    upper = jnp.where(placing & (half == 1), 1.0, 0.0).astype(bf16)
    sent = dot(lower, grad_ref[:, :width], ((1,), (0,))) + dot(upper, grad_ref[:, width:], ((1,), (0,)))
    send_ref[...] = sent.astype(bf16).reshape(send_ref.shape)


def place_inputs_kernel(placing_ref, low_ref, high_ref, send_ref, back_ref):
    placing = placing_ref[...]
    half = half_of(placing.shape)
    zero = jnp.zeros_like(placing)
    lower = jnp.where(half == 0, placing, zero)
    upper = jnp.where(half == 1, placing, zero)

    @pl.when(pl.program_id(0) == 0)
    def _():
        back_ref[: lower.shape[1]] = lower.astype(f32).T.astype(bf16)
        back_ref[lower.shape[1] :] = upper.astype(f32).T.astype(bf16)

    sent = dot(lower, low_ref[...], ((1,), (0,))) + dot(upper, high_ref[...], ((1,), (0,)))
    send_ref[...] = sent.astype(bf16).reshape(send_ref.shape)


def both_halves(x):
    blocks = x.reshape(x.shape[0] // group, group, x.shape[1])
    return (blocks + pltpu.roll(blocks, row_limit, 1)).reshape(x.shape)


def coef_kernel(grad_ref, up_ref, coef_ref, compact_ref):
    grads = grad_ref[...].reshape(coef_ref.shape[0], grad_ref.shape[2])
    width = grad_ref.shape[2]
    low = dot(grads, up_ref[:, :width], ((1,), (1,)))
    high = dot(grads, up_ref[:, width:], ((1,), (1,)))
    part = jnp.where(half_of(low.shape) == 0, low, high)
    coef = (adapter_scale * both_halves(part)).astype(bf16)
    coef_ref[...] = coef
    shape = (coef.shape[0], compact_ref.shape[1])
    row, column = iota(shape, 0), iota(shape, 1)
    first = row // group * group + row % row_limit == column // row_limit * group + column % row_limit
    picked = jnp.where(first & (half_of(shape) == 0), 1.0, 0.0).astype(bf16)
    compact_ref[...] = dot(coef, picked, ((0,), (0,))).astype(bf16)


def term_kernel(place_ref, coef_ref, *refs):
    sections, rank, columns = coef_ref.shape
    lows, highs, out_ref, wide_ref = refs[:sections], refs[sections : 2 * sections], refs[-2], refs[-1]

    @pl.when(pl.program_id(0) == 0)
    def _():
        place = place_ref[0]
        parts = []
        for step in range(sections):
            part = coef_ref[(place + step) % sections]
            parts.append(jnp.where(place + step < sections, part, jnp.zeros_like(part)))
        shape = (columns, wide_ref.shape[0])
        column, row = iota(shape, 0), iota(shape, 1)
        same = column == row // group * row_limit + row % row_limit
        spread = jnp.where(same, 1.0, 0.0).astype(bf16)
        wide = dot(jnp.concatenate(parts, axis=0), spread, ((1,), (0,)))
        wide_ref[...] = wide.T.astype(bf16)

    coef = wide_ref[...]
    low = dot(coef, jnp.concatenate([r[...] for r in lows], axis=0), ((1,), (0,)))
    high = dot(coef, jnp.concatenate([r[...] for r in highs], axis=0), ((1,), (0,)))
    out = jnp.where(half_of(low.shape) == 0, low, high)
    out_ref[...] = out.astype(bf16).reshape(out_ref.shape)


def weight_gradient_kernel(rows_ref, grads_ref, coef_ref, down_ref, grad_down_ref, grad_up_ref):
    slots = coef_ref.shape[0]
    rank = coef_ref.shape[1]
    width = rows_ref.shape[2]
    out_width = grads_ref.shape[2]
    rows = rows_ref[...].reshape(slots, width)
    grads = grads_ref[...].reshape(slots, out_width)
    half = half_of((slots, rank))
    coef = coef_ref[...]
    zero = jnp.zeros_like(coef)
    pair = jnp.concatenate([jnp.where(half == 0, coef, zero), jnp.where(half == 1, coef, zero)], axis=1)
    down = dot(pair, rows, ((0,), (0,)))
    grad_down_ref[:, :width] = down[:rank]
    grad_down_ref[:, width:] = down[rank:]
    low = dot(rows, down_ref[:, :width], ((1,), (1,)))
    high = dot(rows, down_ref[:, width:], ((1,), (1,)))
    proj = both_halves(jnp.where(half == 0, low, high)).astype(bf16)
    pair = jnp.concatenate([jnp.where(half == 0, proj, zero), jnp.where(half == 1, proj, zero)], axis=1)
    up = dot(pair, grads, ((0,), (0,)))
    grad_up_ref[:, :out_width] = up[:rank]
    grad_up_ref[:, out_width:] = up[rank:]


def unplace_kernel(back_ref, rows_ref, out_ref):
    tok_rows = out_ref.shape[0]
    block = rows_ref.shape[2]
    rows = rows_ref[...].reshape(back_ref.shape[1], block)
    both = dot(back_ref[...], rows, ((1,), (0,))).astype(bf16)
    start = pl.multiple_of(pl.program_id(0) * block, block)
    out_ref[:, pl.ds(start, block)] = both[:tok_rows]
    start = pl.multiple_of(out_ref.shape[1] // 2 + pl.program_id(0) * block, block)
    out_ref[:, pl.ds(start, block)] = both[tok_rows:]


def ring_round(blocks, axis):
    count = lax.axis_size(axis)
    down = [(i, (i - 1) % count) for i in range(count)]
    up = [(i, (i + 1) % count) for i in range(count)]
    step = (len(blocks) + 1) // 2
    new = dict(blocks)
    new[step] = lax.ppermute(blocks[step - 1], axis, down)
    if step < count - step:
        new[count - step] = lax.ppermute(blocks[(count - step + 1) % count], axis, up)
    return new


def local(
    layer_input_rows,
    output_gradient,
    tenant,
    adapter_owner_index,
    adapter_down_weight,
    adapter_up_weight,
):
    inputs = layer_input_rows[0]
    gradient_list = output_gradient[0]
    tok_rows, width = inputs.shape
    out_width = gradient_list.shape[1]
    owners = adapter_owner_index.shape[0]
    rank = adapter_up_weight.shape[2]
    slots = owners * group
    sections = lax.axis_size("segment")
    place = lax.axis_index("segment").astype(jnp.int32).reshape(1)
    down_factor = adapter_down_weight[0, 0].T
    up_factor = adapter_up_weight[0, 0]
    half_width = width // 2
    steps = 4
    block = half_width // steps
    shape = jax.ShapeDtypeStruct

    placing, send_grads = pl.pallas_call(
        place_gradient_kernel,
        out_shape=(shape((slots, tok_rows), bf16), shape((owners, group, out_width // 2), bf16)),
        name="place_gradient",
    )(tenant.reshape(1, tok_rows), adapter_owner_index.reshape(1, owners), gradient_list)
    recv_grads = lax.all_to_all(send_grads, "owner", split_axis=0, concat_axis=0, tiled=True)

    send_inputs, back = pl.pallas_call(
        place_inputs_kernel,
        grid=(steps,),
        in_specs=[
            pl.BlockSpec((slots, tok_rows), lambda c: (0, 0)),
            pl.BlockSpec((tok_rows, block), lambda c: (0, c)),
            pl.BlockSpec((tok_rows, block), lambda c: (0, c + steps)),
        ],
        out_specs=(
            pl.BlockSpec((owners, group, block), lambda c: (0, 0, c)),
            pl.BlockSpec((2 * tok_rows, slots), lambda c: (0, 0)),
        ),
        out_shape=(shape((owners, group, half_width), bf16), shape((2 * tok_rows, slots), bf16)),
        name="place_inputs",
    )(placing, inputs, inputs)

    blocks = ring_round(ring_round({0: down_factor}, "segment"), "segment")
    send_inputs, blocks = lax.optimization_barrier((send_inputs, blocks))

    coef, compact = pl.pallas_call(
        coef_kernel,
        out_shape=(shape((slots, rank), bf16), shape((rank, slots // 2), bf16)),
        name="coef",
    )(recv_grads, up_factor)

    recv_inputs = lax.all_to_all(send_inputs, "owner", split_axis=0, concat_axis=0, tiled=True)
    all_coef = lax.all_gather(compact, "segment")
    while len(blocks) < sections:
        blocks = ring_round(blocks, "segment")
    downs = [blocks[step] for step in range(sections)]

    terms = pl.pallas_call(
        term_kernel,
        grid=(steps,),
        in_specs=[
            pl.BlockSpec(memory_space=pltpu.SMEM),
            pl.BlockSpec((sections, rank, slots // 2), lambda c: (0, 0, 0)),
        ]
        + [pl.BlockSpec((rank, block), lambda c: (0, c))] * sections
        + [pl.BlockSpec((rank, block), lambda c: (0, c + steps))] * sections,
        out_specs=pl.BlockSpec((owners, group, block), lambda c: (0, 0, c)),
        out_shape=shape((owners, group, half_width), bf16),
        scratch_shapes=[pltpu.VMEM((slots, sections * rank), bf16)],
        name="term",
    )(place, all_coef, *downs, *downs)
    returned = lax.all_to_all(terms, "owner", split_axis=0, concat_axis=0, tiled=True)

    grad_down, grad_up = pl.pallas_call(
        weight_gradient_kernel,
        out_shape=(shape((rank, width), f32), shape((rank, out_width), f32)),
        name="weight_gradient",
    )(recv_inputs, recv_grads, coef, down_factor)

    passed = pl.pallas_call(
        unplace_kernel,
        grid=(steps,),
        in_specs=[
            pl.BlockSpec((2 * tok_rows, slots), lambda c: (0, 0)),
            pl.BlockSpec((owners, group, block), lambda c: (0, 0, c)),
        ],
        out_specs=pl.BlockSpec((tok_rows, width), lambda c: (0, 0)),
        out_shape=shape((tok_rows, width), bf16),
        name="unplace",
    )(back, returned)

    return (passed[None], grad_down.T[None, None], grad_up[None, None])


def solution(mesh):
    return jax.shard_map(
        local,
        mesh=mesh,
        in_specs=(
            P("segment", "owner", None),
            P("segment", "owner", None),
            P("owner", None),
            P(),
            P("segment", "owner", None, None),
            P("segment", "owner", None, None),
        ),
        out_specs=(
            P("segment", "owner", None),
            P("segment", "owner", None, None),
            P("segment", "owner", None, None),
        ),
        check_vma=False,
    )
```

```python
import jax
import jax.numpy as jnp
from jax import lax
from jax.experimental import pallas as pl
from jax.experimental.pallas import tpu as pltpu
from jax.sharding import PartitionSpec as P

adapter_scale = 2.0
row_limit = 4
group = 2 * row_limit
f32 = jnp.float32
bf16 = jnp.bfloat16


def dot(a, b, contract):
    return lax.dot_general(a, b, (contract, ((), ())), preferred_element_type=f32)


def iota(shape, axis):
    return lax.broadcasted_iota(jnp.int32, shape, axis)


def half_of(shape):
    return (iota(shape, 0) // row_limit) % 2


def place_gradient_kernel(tenant_ref, owner_ref, grad_ref, placing_ref, send_ref):
    tok_rows = tenant_ref.shape[1]
    owners = owner_ref.shape[1]
    slots = owners * group
    named = iota((owners, tok_rows), 0) == tenant_ref[...]
    before = (iota((tok_rows, tok_rows), 0) < iota((tok_rows, tok_rows), 1)).astype(bf16)
    rank = dot(named.astype(bf16), before, ((1,), (0,)))
    key = jnp.where(named, rank + 1.0, 0.0).astype(bf16)
    held = (iota((slots, owners), 0) // group == owner_ref[...]).astype(bf16)
    wide_key = dot(held, key, ((1,), (0,)))
    index = (iota((slots, tok_rows), 0) % row_limit + 1).astype(f32)
    placing = wide_key == index
    placing_ref[...] = placing.astype(bf16)
    half = half_of((slots, tok_rows))
    width = grad_ref.shape[1] // 2
    lower = jnp.where(placing & (half == 0), 1.0, 0.0).astype(bf16)
    upper = jnp.where(placing & (half == 1), 1.0, 0.0).astype(bf16)
    sent = dot(lower, grad_ref[:, :width], ((1,), (0,))) + dot(upper, grad_ref[:, width:], ((1,), (0,)))
    send_ref[...] = sent.astype(bf16).reshape(send_ref.shape)


def place_inputs_kernel(placing_ref, low_ref, high_ref, send_ref, back_ref):
    placing = placing_ref[...]
    half = half_of(placing.shape)
    zero = jnp.zeros_like(placing)
    lower = jnp.where(half == 0, placing, zero)
    upper = jnp.where(half == 1, placing, zero)

    @pl.when(pl.program_id(0) == 0)
    def _():
        back_ref[: lower.shape[1]] = lower.astype(f32).T.astype(bf16)
        back_ref[lower.shape[1] :] = upper.astype(f32).T.astype(bf16)

    sent = dot(lower, low_ref[...], ((1,), (0,))) + dot(upper, high_ref[...], ((1,), (0,)))
    send_ref[...] = sent.astype(bf16).reshape(send_ref.shape)


def both_halves(x):
    blocks = x.reshape(x.shape[0] // group, group, x.shape[1])
    return (blocks + pltpu.roll(blocks, row_limit, 1)).reshape(x.shape)


def coef_kernel(grad_ref, up_ref, coef_ref, compact_ref):
    grads = grad_ref[...].reshape(coef_ref.shape[0], grad_ref.shape[2])
    width = grad_ref.shape[2]
    low = dot(grads, up_ref[:, :width], ((1,), (1,)))
    high = dot(grads, up_ref[:, width:], ((1,), (1,)))
    part = jnp.where(half_of(low.shape) == 0, low, high)
    coef = (adapter_scale * both_halves(part)).astype(bf16)
    coef_ref[...] = coef
    shape = (coef.shape[0], compact_ref.shape[1])
    row, column = iota(shape, 0), iota(shape, 1)
    first = row // group * group + row % row_limit == column // row_limit * group + column % row_limit
    picked = jnp.where(first & (half_of(shape) == 0), 1.0, 0.0).astype(bf16)
    compact_ref[...] = dot(coef, picked, ((0,), (0,))).astype(bf16)


def term_kernel(place_ref, coef_ref, low_ref, high_ref, out_ref, wide_ref):
    sections, rank, columns = coef_ref.shape

    @pl.when(pl.program_id(0) == 0)
    def _():
        place = place_ref[0]
        parts = []
        for k in range(sections):
            parts.append(jnp.where(place <= k, coef_ref[k], jnp.zeros_like(coef_ref[k])))
        shape = (columns, wide_ref.shape[0])
        column, row = iota(shape, 0), iota(shape, 1)
        same = column == row // group * row_limit + row % row_limit
        spread = jnp.where(same, 1.0, 0.0).astype(bf16)
        wide = dot(jnp.concatenate(parts, axis=0), spread, ((1,), (0,)))
        wide_ref[...] = wide.T.astype(bf16)

    coef = wide_ref[...]
    low = dot(coef, low_ref[...], ((1,), (0,)))
    high = dot(coef, high_ref[...], ((1,), (0,)))
    out = jnp.where(half_of(low.shape) == 0, low, high)
    out_ref[...] = out.astype(bf16).reshape(out_ref.shape)


def weight_gradient_kernel(rows_ref, grads_ref, coef_ref, down_ref, grad_down_ref, grad_up_ref):
    slots = coef_ref.shape[0]
    rank = coef_ref.shape[1]
    width = rows_ref.shape[2]
    out_width = grads_ref.shape[2]
    rows = rows_ref[...].reshape(slots, width)
    grads = grads_ref[...].reshape(slots, out_width)
    half = half_of((slots, rank))
    coef = coef_ref[...]
    zero = jnp.zeros_like(coef)
    pair = jnp.concatenate([jnp.where(half == 0, coef, zero), jnp.where(half == 1, coef, zero)], axis=1)
    down = dot(pair, rows, ((0,), (0,)))
    grad_down_ref[:, :width] = down[:rank]
    grad_down_ref[:, width:] = down[rank:]
    low = dot(rows, down_ref[:, :width], ((1,), (1,)))
    high = dot(rows, down_ref[:, width:], ((1,), (1,)))
    proj = both_halves(jnp.where(half == 0, low, high)).astype(bf16)
    pair = jnp.concatenate([jnp.where(half == 0, proj, zero), jnp.where(half == 1, proj, zero)], axis=1)
    up = dot(pair, grads, ((0,), (0,)))
    grad_up_ref[:, :out_width] = up[:rank]
    grad_up_ref[:, out_width:] = up[rank:]


def unplace_kernel(back_ref, rows_ref, out_ref):
    tok_rows = out_ref.shape[0]
    block = rows_ref.shape[2]
    rows = rows_ref[...].reshape(back_ref.shape[1], block)
    both = dot(back_ref[...], rows, ((1,), (0,))).astype(bf16)
    start = pl.multiple_of(pl.program_id(0) * block, block)
    out_ref[:, pl.ds(start, block)] = both[:tok_rows]
    start = pl.multiple_of(out_ref.shape[1] // 2 + pl.program_id(0) * block, block)
    out_ref[:, pl.ds(start, block)] = both[tok_rows:]


def local(
    layer_input_rows,
    output_gradient,
    tenant,
    adapter_owner_index,
    adapter_down_weight,
    adapter_up_weight,
):
    inputs = layer_input_rows[0]
    gradient_list = output_gradient[0]
    tok_rows, width = inputs.shape
    out_width = gradient_list.shape[1]
    owners = adapter_owner_index.shape[0]
    rank = adapter_up_weight.shape[2]
    slots = owners * group
    sections = lax.axis_size("segment")
    place = lax.axis_index("segment").astype(jnp.int32).reshape(1)
    down_factor = adapter_down_weight[0, 0].T
    up_factor = adapter_up_weight[0, 0]
    half_width = width // 2
    steps = 4
    block = half_width // steps
    shape = jax.ShapeDtypeStruct

    all_down = lax.all_gather(down_factor, "segment").reshape(sections * rank, width)

    placing, send_grads = pl.pallas_call(
        place_gradient_kernel,
        out_shape=(shape((slots, tok_rows), bf16), shape((owners, group, out_width // 2), bf16)),
        name="place_gradient",
    )(tenant.reshape(1, tok_rows), adapter_owner_index.reshape(1, owners), gradient_list)
    recv_grads = lax.all_to_all(send_grads, "owner", split_axis=0, concat_axis=0, tiled=True)

    send_inputs, back = pl.pallas_call(
        place_inputs_kernel,
        grid=(steps,),
        in_specs=[
            pl.BlockSpec((slots, tok_rows), lambda c: (0, 0)),
            pl.BlockSpec((tok_rows, block), lambda c: (0, c)),
            pl.BlockSpec((tok_rows, block), lambda c: (0, c + steps)),
        ],
        out_specs=(
            pl.BlockSpec((owners, group, block), lambda c: (0, 0, c)),
            pl.BlockSpec((2 * tok_rows, slots), lambda c: (0, 0)),
        ),
        out_shape=(shape((owners, group, half_width), bf16), shape((2 * tok_rows, slots), bf16)),
        name="place_inputs",
    )(placing, inputs, inputs)

    coef, compact = pl.pallas_call(
        coef_kernel,
        out_shape=(shape((slots, rank), bf16), shape((rank, slots // 2), bf16)),
        name="coef",
    )(recv_grads, up_factor)

    recv_inputs = lax.all_to_all(send_inputs, "owner", split_axis=0, concat_axis=0, tiled=True)
    all_coef = lax.all_gather(compact, "segment")

    terms = pl.pallas_call(
        term_kernel,
        grid=(steps,),
        in_specs=[
            pl.BlockSpec(memory_space=pltpu.SMEM),
            pl.BlockSpec((sections, rank, slots // 2), lambda c: (0, 0, 0)),
            pl.BlockSpec((sections * rank, block), lambda c: (0, c)),
            pl.BlockSpec((sections * rank, block), lambda c: (0, c + steps)),
        ],
        out_specs=pl.BlockSpec((owners, group, block), lambda c: (0, 0, c)),
        out_shape=shape((owners, group, half_width), bf16),
        scratch_shapes=[pltpu.VMEM((slots, sections * rank), bf16)],
        name="term",
    )(place, all_coef, all_down, all_down)
    returned = lax.all_to_all(terms, "owner", split_axis=0, concat_axis=0, tiled=True)

    grad_down, grad_up = pl.pallas_call(
        weight_gradient_kernel,
        out_shape=(shape((rank, width), f32), shape((rank, out_width), f32)),
        name="weight_gradient",
    )(recv_inputs, recv_grads, coef, down_factor)

    passed = pl.pallas_call(
        unplace_kernel,
        grid=(steps,),
        in_specs=[
            pl.BlockSpec((2 * tok_rows, slots), lambda c: (0, 0)),
            pl.BlockSpec((owners, group, block), lambda c: (0, 0, c)),
        ],
        out_specs=pl.BlockSpec((tok_rows, width), lambda c: (0, 0)),
        out_shape=shape((tok_rows, width), bf16),
        name="unplace",
    )(back, returned)

    return (passed[None], grad_down.T[None, None], grad_up[None, None])


def solution(mesh):
    return jax.shard_map(
        local,
        mesh=mesh,
        in_specs=(
            P("segment", "owner", None),
            P("segment", "owner", None),
            P("owner", None),
            P(),
            P("segment", "owner", None, None),
            P("segment", "owner", None, None),
        ),
        out_specs=(
            P("segment", "owner", None),
            P("segment", "owner", None, None),
            P("segment", "owner", None, None),
        ),
        check_vma=False,
    )
```

```python
import jax
import jax.numpy as jnp
from jax import lax
from jax.experimental import pallas as pl
from jax.experimental.pallas import tpu as pltpu
from jax.sharding import PartitionSpec as P

adapter_scale = 2.0
row_limit = 4
group = 2 * row_limit
banks = 8
members = 8
bank_slots = 23
lines = 2 * bank_slots + 2
f32 = jnp.float32
bf16 = jnp.bfloat16


def dot(a, b, contract):
    return lax.dot_general(a, b, (contract, ((), ())), preferred_element_type=f32)


def iota(shape, axis):
    return lax.broadcasted_iota(jnp.int32, shape, axis)


def half_of(shape):
    return (iota(shape, 0) // row_limit) % 2


def place_gradient_kernel(tenant_ref, owner_ref, grad_ref, placing_ref, send_ref):
    tok_rows = tenant_ref.shape[1]
    owners = owner_ref.shape[1]
    slots = owners * group
    named = iota((owners, tok_rows), 0) == tenant_ref[...]
    before = (iota((tok_rows, tok_rows), 0) < iota((tok_rows, tok_rows), 1)).astype(bf16)
    rank = dot(named.astype(bf16), before, ((1,), (0,)))
    key = jnp.where(named, rank + 1.0, 0.0).astype(bf16)
    held = (iota((slots, owners), 0) // group == owner_ref[...]).astype(bf16)
    wide_key = dot(held, key, ((1,), (0,)))
    index = (iota((slots, tok_rows), 0) % row_limit + 1).astype(f32)
    placing = wide_key == index
    placing_ref[...] = placing.astype(bf16)
    half = half_of((slots, tok_rows))
    width = grad_ref.shape[1] // 2
    lower = jnp.where(placing & (half == 0), 1.0, 0.0).astype(bf16)
    upper = jnp.where(placing & (half == 1), 1.0, 0.0).astype(bf16)
    sent = dot(lower, grad_ref[:, :width], ((1,), (0,))) + dot(upper, grad_ref[:, width:], ((1,), (0,)))
    send_ref[...] = sent.astype(bf16).reshape(send_ref.shape)


def place_inputs_kernel(placing_ref, low_ref, high_ref, send_ref):
    placing = placing_ref[...]
    half = half_of(placing.shape)
    zero = jnp.zeros_like(placing)
    lower = jnp.where(half == 0, placing, zero)
    upper = jnp.where(half == 1, placing, zero)
    sent = dot(lower, low_ref[...], ((1,), (0,))) + dot(upper, high_ref[...], ((1,), (0,)))
    send_ref[...] = sent.astype(bf16).reshape(send_ref.shape)


def place_banks_kernel(tenant_ref, owner_ref, placing_ref, low_ref, high_ref, send_ref, back_ref, pick_ref, code_ref):
    tok_rows = tenant_ref.shape[1]
    owners = owner_ref.shape[1]
    total = banks * lines
    block = low_ref.shape[1]
    step = pl.program_id(0)

    @pl.when(step == 0)
    def _():
        placing = placing_ref[...].astype(f32)
        half = half_of(placing.shape)
        back_ref[:tok_rows] = jnp.where(half == 0, placing, 0.0).T.astype(bf16)
        back_ref[tok_rows:] = jnp.where(half == 1, placing, 0.0).T.astype(bf16)
        named = iota((owners, tok_rows), 0) == tenant_ref[...]
        named_bf16 = named.astype(bf16)
        before = (iota((tok_rows, tok_rows), 0) < iota((tok_rows, tok_rows), 1)).astype(bf16)
        in_bank = dot((iota((banks, owners), 0) == owner_ref[...] // members).astype(bf16), named_bf16, ((1,), (0,)))
        bank_rank = dot(in_bank.astype(bf16), before, ((1,), (0,)))
        key = in_bank * (bank_rank + 1.0)
        most = jnp.max(key)
        slot = jnp.sum(key, axis=0, keepdims=True) - 1.0
        rank = dot(named_bf16, before, ((1,), (0,)))
        place = jnp.sum(jnp.where(named, rank, 0.0), axis=0, keepdims=True)
        member = jnp.broadcast_to((owner_ref[...] % members).astype(f32), (banks, owners)).astype(bf16)
        member = dot(member, named_bf16, ((1,), (0,)))
        code = in_bank * (member * row_limit + place + 1.0)
        line = iota((tok_rows, tok_rows), 0)
        mine = ((line % bank_slots).astype(f32) == slot) & (line < 2 * bank_slots)
        codes = dot(code.astype(bf16), mine.astype(bf16), ((1,), (1,)))
        spread = (iota((total, banks), 0) // lines == iota((total, banks), 1)).astype(bf16)
        wide_key = dot(spread, key.astype(bf16), ((1,), (0,)))
        line = iota((total, tok_rows), 0) % lines
        pick = (wide_key == (line % bank_slots + 1).astype(f32)) & (line < 2 * bank_slots)
        pick_ref[0] = jnp.where(pick & (line < bank_slots), 1.0, 0.0).astype(bf16)
        pick_ref[1] = jnp.where(pick & (line >= bank_slots), 1.0, 0.0).astype(bf16)
        wide_code = dot(spread, codes.astype(bf16), ((1,), (0,)))
        code_ref[...] = jnp.where(line == lines - 2, wide_code, jnp.where(line == lines - 1, most, 0.0))

    sent = dot(pick_ref[0], low_ref[...], ((1,), (0,))) + dot(pick_ref[1], high_ref[...], ((1,), (0,)))
    send_ref[...] = sent.astype(bf16).reshape(send_ref.shape)

    @pl.when(step == 0)
    def _():
        first = sent[:, :tok_rows] + code_ref[...]
        send_ref[:, :, :tok_rows] = first.astype(bf16).reshape(banks, lines, tok_rows)


def route_kernel(member_ref, rows_ref, *refs):
    outs, pick_ref, most_ref = refs[:members], refs[members], refs[members + 1]
    block = rows_ref.shape[2]
    rows = members * group

    @pl.when(pl.program_id(0) == 0)
    def _():
        x, core = member_ref[0] // 2, member_ref[0] % 2
        row, line = iota((rows, lines), 0), iota((rows, lines), 1)
        t = row // group
        to = (x + t // 2) % 4 * 2 + (core + t) % 2
        want = (to * row_limit + row % row_limit + 1).astype(f32)
        same_half = (row // row_limit) % 2 == line // bank_slots
        most = jnp.zeros((1, 128), f32)
        for y in range(banks):
            tail = rows_ref[y, :, :128].astype(f32)
            codes = tail[lines - 2 : lines - 1, :lines]
            most = jnp.maximum(most, tail[lines - 1 :, :])
            pick_ref[y] = jnp.where((want == codes) & same_half, 1.0, 0.0).astype(bf16)
        most_ref[...] = jnp.broadcast_to(most, most_ref.shape)

    for y in range(banks):
        part = dot(pick_ref[y], rows_ref[y], ((1,), (0,))).astype(bf16).reshape(members, group, block)
        for t in range(members):
            outs[t][y] = part[t]
    most = jnp.broadcast_to(most_ref[:, :1], (group, block)).astype(bf16)
    for t in range(members):
        outs[t][banks] = most


def both_halves(x):
    blocks = x.reshape(x.shape[0] // group, group, x.shape[1])
    return (blocks + pltpu.roll(blocks, row_limit, 1)).reshape(x.shape)


def coef_kernel(grad_ref, up_ref, coef_ref, compact_ref):
    grads = grad_ref[...].reshape(coef_ref.shape[0], grad_ref.shape[2])
    width = grad_ref.shape[2]
    low = dot(grads, up_ref[:, :width], ((1,), (1,)))
    high = dot(grads, up_ref[:, width:], ((1,), (1,)))
    part = jnp.where(half_of(low.shape) == 0, low, high)
    coef = (adapter_scale * both_halves(part)).astype(bf16)
    coef_ref[...] = coef
    shape = (coef.shape[0], compact_ref.shape[1])
    row, column = iota(shape, 0), iota(shape, 1)
    first = row // group * group + row % row_limit == column // row_limit * group + column % row_limit
    picked = jnp.where(first & (half_of(shape) == 0), 1.0, 0.0).astype(bf16)
    compact_ref[...] = dot(coef, picked, ((0,), (0,))).astype(bf16)


def term_kernel(place_ref, coef_ref, low_ref, high_ref, out_ref, wide_ref):
    sections, rank, columns = coef_ref.shape

    @pl.when(pl.program_id(0) == 0)
    def _():
        place = place_ref[0]
        parts = []
        for k in range(sections):
            part = coef_ref[jnp.bitwise_xor(place, k)]
            parts.append(jnp.where(place <= k, part, jnp.zeros_like(part)))
        shape = (columns, wide_ref.shape[0])
        column, row = iota(shape, 0), iota(shape, 1)
        same = column == row // group * row_limit + row % row_limit
        spread = jnp.where(same, 1.0, 0.0).astype(bf16)
        wide = dot(jnp.concatenate(parts, axis=0), spread, ((1,), (0,)))
        wide_ref[...] = wide.T.astype(bf16)

    coef = wide_ref[...]
    low = dot(coef, low_ref[...], ((1,), (0,)))
    high = dot(coef, high_ref[...], ((1,), (0,)))
    out = jnp.where(half_of(low.shape) == 0, low, high)
    out_ref[...] = out.astype(bf16).reshape(out_ref.shape)


def gradients(rows, grads, coef, down_ref, grad_down_ref, grad_up_ref):
    rank = coef.shape[1]
    width = rows.shape[1]
    out_width = grads.shape[1]
    half = half_of(coef.shape)
    zero = jnp.zeros_like(coef)
    pair = jnp.concatenate([jnp.where(half == 0, coef, zero), jnp.where(half == 1, coef, zero)], axis=1)
    down = dot(pair, rows, ((0,), (0,)))
    grad_down_ref[:, :width] = down[:rank]
    grad_down_ref[:, width:] = down[rank:]
    low = dot(rows, down_ref[:, :width], ((1,), (1,)))
    high = dot(rows, down_ref[:, width:], ((1,), (1,)))
    proj = both_halves(jnp.where(half == 0, low, high)).astype(bf16)
    pair = jnp.concatenate([jnp.where(half == 0, proj, zero), jnp.where(half == 1, proj, zero)], axis=1)
    up = dot(pair, grads, ((0,), (0,)))
    grad_up_ref[:, :out_width] = up[:rank]
    grad_up_ref[:, out_width:] = up[rank:]


def weight_gradient_kernel(rows_ref, grads_ref, coef_ref, down_ref, grad_down_ref, grad_up_ref):
    slots = coef_ref.shape[0]
    rows = rows_ref[...].reshape(slots, rows_ref.shape[2])
    grads = grads_ref[...].reshape(slots, grads_ref.shape[2])
    gradients(rows, grads, coef_ref[...], down_ref, grad_down_ref, grad_up_ref)


def bank_gradient_kernel(member_ref, grads_ref, coef_ref, down_ref, *refs):
    blocks, (grad_down_ref, grad_up_ref, most_ref) = refs[:members], refs[members:]
    rank = coef_ref.shape[3]
    out_width = grads_ref.shape[3]
    width = down_ref.shape[1] // 2
    x, core = member_ref[0] // 2, member_ref[0] % 2
    rows, coef, grads = [], [], []
    most = jnp.zeros((group, 128), f32)
    for t in range(members):
        source = (x + 4 - t // 2) % 4 * 2 + (core + t) % 2
        rows.append(blocks[t][:banks].reshape(banks * group, width))
        coef.append(coef_ref[:, pl.ds(source, 1)].reshape(banks * group, rank))
        grads.append(grads_ref[:, pl.ds(source, 1)].reshape(banks * group, out_width))
        most = jnp.maximum(most, blocks[t][banks, :, :128].astype(f32))
    most_ref[0] = jnp.max(most).astype(jnp.int32)
    rows, coef, grads = (jnp.concatenate(part, axis=0) for part in (rows, coef, grads))
    gradients(rows, grads, coef, down_ref, grad_down_ref, grad_up_ref)


def unplace_kernel(back_ref, rows_ref, out_ref):
    tok_rows = out_ref.shape[0]
    block = rows_ref.shape[2]
    rows = rows_ref[...].reshape(back_ref.shape[1], block)
    both = dot(back_ref[...], rows, ((1,), (0,))).astype(bf16)
    start = pl.multiple_of(pl.program_id(0) * block, block)
    out_ref[:, pl.ds(start, block)] = both[:tok_rows]
    start = pl.multiple_of(out_ref.shape[1] // 2 + pl.program_id(0) * block, block)
    out_ref[:, pl.ds(start, block)] = both[tok_rows:]


def local(
    layer_input_rows,
    output_gradient,
    tenant,
    adapter_owner_index,
    adapter_down_weight,
    adapter_up_weight,
):
    inputs = layer_input_rows[0]
    gradient_list = output_gradient[0]
    tok_rows, width = inputs.shape
    out_width = gradient_list.shape[1]
    owners = adapter_owner_index.shape[0]
    rank = adapter_up_weight.shape[2]
    slots = owners * group
    sections = lax.axis_size("segment")
    place = lax.axis_index("segment").astype(jnp.int32).reshape(1)
    down_factor = adapter_down_weight[0, 0].T
    up_factor = adapter_up_weight[0, 0]
    half_width = width // 2
    steps = 4
    block = half_width // steps
    shape = jax.ShapeDtypeStruct

    all_down = lax.all_gather(down_factor, "segment").reshape(sections * rank, width)

    owner_row = adapter_owner_index.reshape(1, owners)
    tenant_row = tenant.reshape(1, tok_rows)
    member = (lax.axis_index("owner") % members).astype(jnp.int32).reshape(1)

    placing, send_grads = pl.pallas_call(
        place_gradient_kernel,
        out_shape=(shape((slots, tok_rows), bf16), shape((owners, group, out_width // 2), bf16)),
        name="place_gradient",
    )(tenant_row, owner_row, gradient_list)
    recv_grads = lax.all_to_all(send_grads, "owner", split_axis=0, concat_axis=0, tiled=True)

    send_banks, back = pl.pallas_call(
        place_banks_kernel,
        grid=(steps,),
        in_specs=[
            pl.BlockSpec((1, tok_rows), lambda c: (0, 0)),
            pl.BlockSpec((1, owners), lambda c: (0, 0)),
            pl.BlockSpec((slots, tok_rows), lambda c: (0, 0)),
            pl.BlockSpec((tok_rows, block), lambda c: (0, c)),
            pl.BlockSpec((tok_rows, block), lambda c: (0, c + steps)),
        ],
        out_specs=(
            pl.BlockSpec((banks, lines, block), lambda c: (0, 0, c)),
            pl.BlockSpec((2 * tok_rows, slots), lambda c: (0, 0)),
        ),
        out_shape=(shape((banks, lines, half_width), bf16), shape((2 * tok_rows, slots), bf16)),
        scratch_shapes=[pltpu.VMEM((2, banks * lines, tok_rows), bf16), pltpu.VMEM((banks * lines, tok_rows), f32)],
        name="place_banks",
    )(tenant_row, owner_row, placing, inputs, inputs)

    coef, compact = pl.pallas_call(
        coef_kernel,
        out_shape=(shape((slots, rank), bf16), shape((rank, slots // 2), bf16)),
        name="coef",
    )(recv_grads, up_factor)

    same_member = [[y * members + m for y in range(banks)] for m in range(members)]
    recv_banks = lax.all_to_all(
        send_banks, "owner", split_axis=0, concat_axis=0, axis_index_groups=same_member, tiled=True
    )
    all_coef = compact[None]
    while all_coef.shape[0] < sections:
        apart = all_coef.shape[0]
        other = lax.ppermute(all_coef, "segment", [(i, i ^ apart) for i in range(sections)])
        all_coef = jnp.concatenate([all_coef, other], axis=0)

    terms = pl.pallas_call(
        term_kernel,
        grid=(steps,),
        in_specs=[
            pl.BlockSpec(memory_space=pltpu.SMEM),
            pl.BlockSpec((sections, rank, slots // 2), lambda c: (0, 0, 0)),
            pl.BlockSpec((sections * rank, block), lambda c: (0, c)),
            pl.BlockSpec((sections * rank, block), lambda c: (0, c + steps)),
        ],
        out_specs=pl.BlockSpec((owners, group, block), lambda c: (0, 0, c)),
        out_shape=shape((owners, group, half_width), bf16),
        scratch_shapes=[pltpu.VMEM((slots, sections * rank), bf16)],
        name="term",
    )(place, all_coef, all_down, all_down)
    returned = lax.all_to_all(terms, "owner", split_axis=0, concat_axis=0, tiled=True)

    sent_blocks = pl.pallas_call(
        route_kernel,
        grid=(steps,),
        in_specs=[
            pl.BlockSpec(memory_space=pltpu.SMEM),
            pl.BlockSpec((banks, lines, block), lambda c: (0, 0, c)),
        ],
        out_specs=[pl.BlockSpec((banks + 1, group, block), lambda c: (0, 0, c))] * members,
        out_shape=[shape((banks + 1, group, half_width), bf16)] * members,
        scratch_shapes=[pltpu.VMEM((banks, members * group, lines), bf16), pltpu.VMEM((group, 128), f32)],
        name="route",
    )(member, recv_banks)
    got_blocks = [sent_blocks[0]]
    for t in range(1, members):
        pairs = []
        for i in range(owners):
            y, x, core = i // members, i % members // 2, i % 2
            pairs.append((i, y * members + (x + t // 2) % 4 * 2 + (core + t) % 2))
        got_blocks.append(lax.ppermute(sent_blocks[t], "owner", pairs))

    smem = pl.BlockSpec(memory_space=pltpu.SMEM)
    vmem = pl.BlockSpec(memory_space=pltpu.VMEM)
    grad_down, grad_up, most = pl.pallas_call(
        bank_gradient_kernel,
        in_specs=[smem] + [vmem] * (3 + members),
        out_specs=(vmem, vmem, smem),
        out_shape=(shape((rank, width), f32), shape((rank, out_width), f32), shape((1,), jnp.int32)),
        name="bank_gradient",
    )(
        member,
        recv_grads.reshape(banks, members, group, out_width // 2),
        coef.reshape(banks, members, group, rank),
        down_factor,
        *got_blocks,
    )

    def direct(grad_down, grad_up, placing, inputs, recv_grads, coef, down_factor):
        send_inputs = pl.pallas_call(
            place_inputs_kernel,
            grid=(steps,),
            in_specs=[
                pl.BlockSpec((slots, tok_rows), lambda c: (0, 0)),
                pl.BlockSpec((tok_rows, block), lambda c: (0, c)),
                pl.BlockSpec((tok_rows, block), lambda c: (0, c + steps)),
            ],
            out_specs=pl.BlockSpec((owners, group, block), lambda c: (0, 0, c)),
            out_shape=shape((owners, group, half_width), bf16),
            name="place_inputs",
        )(placing, inputs, inputs)
        recv_inputs = lax.all_to_all(send_inputs, "owner", split_axis=0, concat_axis=0, tiled=True)
        return tuple(
            pl.pallas_call(
                weight_gradient_kernel,
                out_shape=(shape((rank, width), f32), shape((rank, out_width), f32)),
                name="weight_gradient",
            )(recv_inputs, recv_grads, coef, down_factor)
        )

    def kept(grad_down, grad_up, *rest):
        return grad_down, grad_up

    grad_down, grad_up, most, returned = lax.optimization_barrier((grad_down, grad_up, most, returned))
    grad_down, grad_up = lax.cond(
        most[0] > bank_slots, direct, kept, grad_down, grad_up, placing, inputs, recv_grads, coef, down_factor
    )

    passed = pl.pallas_call(
        unplace_kernel,
        grid=(steps,),
        in_specs=[
            pl.BlockSpec((2 * tok_rows, slots), lambda c: (0, 0)),
            pl.BlockSpec((owners, group, block), lambda c: (0, 0, c)),
        ],
        out_specs=pl.BlockSpec((tok_rows, width), lambda c: (0, 0)),
        out_shape=shape((tok_rows, width), bf16),
        name="unplace",
    )(back, returned)

    return (passed[None], grad_down.T[None, None], grad_up[None, None])


def solution(mesh):
    return jax.shard_map(
        local,
        mesh=mesh,
        in_specs=(
            P("segment", "owner", None),
            P("segment", "owner", None),
            P("owner", None),
            P(),
            P("segment", "owner", None, None),
            P("segment", "owner", None, None),
        ),
        out_specs=(
            P("segment", "owner", None),
            P("segment", "owner", None, None),
            P("segment", "owner", None, None),
        ),
        check_vma=False,
    )
```

```python
import jax
import jax.numpy as jnp
from jax import lax
from jax.experimental import pallas as pl
from jax.experimental.pallas import tpu as pltpu
from jax.sharding import PartitionSpec as P

adapter_scale = 2.0
row_limit = 4
group = 2 * row_limit
pieces = 2
f32 = jnp.float32
bf16 = jnp.bfloat16


def dot(a, b, contract):
    return lax.dot_general(a, b, (contract, ((), ())), preferred_element_type=f32)


def iota(shape, axis):
    return lax.broadcasted_iota(jnp.int32, shape, axis)


def half_of(shape):
    return (iota(shape, 0) // row_limit) % 2


def place_gradient_kernel(tenant_ref, owner_ref, grad_hbm, placing_ref, send_hbm, grad_ref, send_ref, sems):
    read = pltpu.make_async_copy(grad_hbm, grad_ref, sems.at[0])
    read.start()
    tok_rows = tenant_ref.shape[1]
    owners = owner_ref.shape[1]
    slots = owners * group
    named = iota((owners, tok_rows), 0) == tenant_ref[...]
    before = (iota((tok_rows, tok_rows), 0) < iota((tok_rows, tok_rows), 1)).astype(bf16)
    rank = dot(named.astype(bf16), before, ((1,), (0,)))
    key = jnp.where(named, rank + 1.0, 0.0).astype(bf16)
    held = (iota((slots, owners), 0) // group == owner_ref[...]).astype(bf16)
    wide_key = dot(held, key, ((1,), (0,)))
    index = (iota((slots, tok_rows), 0) % row_limit + 1).astype(f32)
    placing = wide_key == index
    placing_ref[...] = placing.astype(bf16)
    half = half_of((slots, tok_rows))
    width = grad_ref.shape[1] // 2
    lower = jnp.where(placing & (half == 0), 1.0, 0.0).astype(bf16)
    upper = jnp.where(placing & (half == 1), 1.0, 0.0).astype(bf16)
    read.wait()
    low, high = grad_ref[:, :width], grad_ref[:, width:]
    part, count = slots // pieces, owners // pieces
    writes = []
    for p in range(pieces):
        rows = slice(p * part, (p + 1) * part)
        sent = dot(lower[rows], low, ((1,), (0,))) + dot(upper[rows], high, ((1,), (0,)))
        here = pl.ds(p * count, count)
        send_ref[here] = sent.astype(bf16).reshape(count, group, width)
        writes.append(pltpu.make_async_copy(send_ref.at[here], send_hbm.at[here], sems.at[1 + p]))
        writes[-1].start()
    for write in writes:
        write.wait()


def place_inputs_kernel(placing_ref, low_ref, high_ref, send_ref, back_ref):
    placing = placing_ref[...]
    half = half_of(placing.shape)
    zero = jnp.zeros_like(placing)
    lower = jnp.where(half == 0, placing, zero)
    upper = jnp.where(half == 1, placing, zero)

    @pl.when(pl.program_id(0) == 0)
    def _():
        back_ref[: lower.shape[1]] = lower.astype(f32).T.astype(bf16)
        back_ref[lower.shape[1] :] = upper.astype(f32).T.astype(bf16)

    sent = dot(lower, low_ref[...], ((1,), (0,))) + dot(upper, high_ref[...], ((1,), (0,)))
    send_ref[...] = sent.astype(bf16).reshape(send_ref.shape)


def both_halves(x):
    blocks = x.reshape(x.shape[0] // group, group, x.shape[1])
    return (blocks + pltpu.roll(blocks, row_limit, 1)).reshape(x.shape)


def coef_kernel(grad_ref, up_ref, coef_ref, compact_ref):
    grads = grad_ref[...].reshape(coef_ref.shape[0], grad_ref.shape[2])
    width = grad_ref.shape[2]
    low = dot(grads, up_ref[:, :width], ((1,), (1,)))
    high = dot(grads, up_ref[:, width:], ((1,), (1,)))
    part = jnp.where(half_of(low.shape) == 0, low, high)
    coef = (adapter_scale * both_halves(part)).astype(bf16)
    coef_ref[...] = coef
    shape = (coef.shape[0], compact_ref.shape[1])
    row, column = iota(shape, 0), iota(shape, 1)
    first = row // group * group + row % row_limit == column // row_limit * group + column % row_limit
    picked = jnp.where(first & (half_of(shape) == 0), 1.0, 0.0).astype(bf16)
    compact_ref[...] = dot(coef, picked, ((0,), (0,))).astype(bf16)


def term_kernel(place_ref, coef_ref, low_ref, high_ref, out_ref, wide_ref):
    sections, rank, columns = coef_ref.shape

    @pl.when(pl.program_id(0) == 0)
    def _():
        place = place_ref[0]
        parts = []
        for k in range(sections):
            parts.append(jnp.where(place <= k, coef_ref[k], jnp.zeros_like(coef_ref[k])))
        shape = (columns, wide_ref.shape[0])
        column, row = iota(shape, 0), iota(shape, 1)
        same = column == row // group * row_limit + row % row_limit
        spread = jnp.where(same, 1.0, 0.0).astype(bf16)
        wide = dot(jnp.concatenate(parts, axis=0), spread, ((1,), (0,)))
        wide_ref[...] = wide.T.astype(bf16)

    coef = wide_ref[...]
    low = dot(coef, low_ref[...], ((1,), (0,)))
    high = dot(coef, high_ref[...], ((1,), (0,)))
    out = jnp.where(half_of(low.shape) == 0, low, high)
    out_ref[...] = out.astype(bf16).reshape(out_ref.shape)


def weight_gradient_kernel(rows_ref, grads_ref, coef_ref, down_ref, grad_down_ref, grad_up_ref):
    slots = coef_ref.shape[0]
    rank = coef_ref.shape[1]
    width = rows_ref.shape[2]
    out_width = grads_ref.shape[2]
    rows = rows_ref[...].reshape(slots, width)
    grads = grads_ref[...].reshape(slots, out_width)
    half = half_of((slots, rank))
    coef = coef_ref[...]
    zero = jnp.zeros_like(coef)
    pair = jnp.concatenate([jnp.where(half == 0, coef, zero), jnp.where(half == 1, coef, zero)], axis=1)
    down = dot(pair, rows, ((0,), (0,)))
    grad_down_ref[:, :width] = down[:rank]
    grad_down_ref[:, width:] = down[rank:]
    low = dot(rows, down_ref[:, :width], ((1,), (1,)))
    high = dot(rows, down_ref[:, width:], ((1,), (1,)))
    proj = both_halves(jnp.where(half == 0, low, high)).astype(bf16)
    pair = jnp.concatenate([jnp.where(half == 0, proj, zero), jnp.where(half == 1, proj, zero)], axis=1)
    up = dot(pair, grads, ((0,), (0,)))
    grad_up_ref[:, :out_width] = up[:rank]
    grad_up_ref[:, out_width:] = up[rank:]


def unplace_kernel(back_ref, rows_ref, out_hbm, out_ref, sems):
    steps = out_ref.shape[0]
    tok_rows = out_hbm.shape[0]
    block = rows_ref.shape[2]
    step = pl.program_id(0)

    def write(c, h):
        start = pl.multiple_of((h * steps + c) * block, block)
        here = out_hbm.at[:, pl.ds(start, block)]
        return pltpu.make_async_copy(out_ref.at[c, pl.ds(h * tok_rows, tok_rows)], here, sems.at[c, h])

    rows = rows_ref[...].reshape(back_ref.shape[1], block)
    out_ref[step] = dot(back_ref[...], rows, ((1,), (0,))).astype(bf16)
    write(step, 0).start()
    write(step, 1).start()

    @pl.when(step == steps - 1)
    def _():
        for c in range(steps):
            write(c, 0).wait()
            write(c, 1).wait()


def local(
    layer_input_rows,
    output_gradient,
    tenant,
    adapter_owner_index,
    adapter_down_weight,
    adapter_up_weight,
):
    inputs = layer_input_rows[0]
    gradient_list = output_gradient[0]
    tok_rows, width = inputs.shape
    out_width = gradient_list.shape[1]
    owners = adapter_owner_index.shape[0]
    rank = adapter_up_weight.shape[2]
    slots = owners * group
    sections = lax.axis_size("segment")
    place = lax.axis_index("segment").astype(jnp.int32).reshape(1)
    down_factor = adapter_down_weight[0, 0].T
    up_factor = adapter_up_weight[0, 0]
    half_width = width // 2
    steps = 4
    block = half_width // steps
    shape = jax.ShapeDtypeStruct

    vmem = pl.BlockSpec(memory_space=pltpu.VMEM)
    anywhere = pl.BlockSpec(memory_space=pl.ANY)

    all_down = lax.all_gather(down_factor, "segment").reshape(sections * rank, width)

    placing, send_grads = pl.pallas_call(
        place_gradient_kernel,
        in_specs=[vmem, vmem, anywhere],
        out_specs=(vmem, anywhere),
        out_shape=(shape((slots, tok_rows), bf16), shape((owners, group, out_width // 2), bf16)),
        scratch_shapes=[
            pltpu.VMEM((tok_rows, out_width), bf16),
            pltpu.VMEM((owners, group, out_width // 2), bf16),
            pltpu.SemaphoreType.DMA((1 + pieces,)),
        ],
        name="place_gradient",
    )(tenant.reshape(1, tok_rows), adapter_owner_index.reshape(1, owners), gradient_list)
    recv_grads = lax.all_to_all(send_grads, "owner", split_axis=0, concat_axis=0, tiled=True)

    send_inputs, back = pl.pallas_call(
        place_inputs_kernel,
        grid=(steps,),
        in_specs=[
            pl.BlockSpec((slots, tok_rows), lambda c: (0, 0)),
            pl.BlockSpec((tok_rows, block), lambda c: (0, c)),
            pl.BlockSpec((tok_rows, block), lambda c: (0, c + steps)),
        ],
        out_specs=(
            pl.BlockSpec((owners, group, block), lambda c: (0, 0, c)),
            pl.BlockSpec((2 * tok_rows, slots), lambda c: (0, 0)),
        ),
        out_shape=(shape((owners, group, half_width), bf16), shape((2 * tok_rows, slots), bf16)),
        name="place_inputs",
    )(placing, inputs, inputs)

    coef, compact = pl.pallas_call(
        coef_kernel,
        out_shape=(shape((slots, rank), bf16), shape((rank, slots // 2), bf16)),
        name="coef",
    )(recv_grads, up_factor)

    recv_inputs = lax.all_to_all(send_inputs, "owner", split_axis=0, concat_axis=0, tiled=True)
    all_coef = lax.all_gather(compact, "segment")

    terms = pl.pallas_call(
        term_kernel,
        grid=(steps,),
        in_specs=[
            pl.BlockSpec(memory_space=pltpu.SMEM),
            pl.BlockSpec((sections, rank, slots // 2), lambda c: (0, 0, 0)),
            pl.BlockSpec((sections * rank, block), lambda c: (0, c)),
            pl.BlockSpec((sections * rank, block), lambda c: (0, c + steps)),
        ],
        out_specs=pl.BlockSpec((owners, group, block), lambda c: (0, 0, c)),
        out_shape=shape((owners, group, half_width), bf16),
        scratch_shapes=[pltpu.VMEM((slots, sections * rank), bf16)],
        name="term",
    )(place, all_coef, all_down, all_down)
    returned = lax.all_to_all(terms, "owner", split_axis=0, concat_axis=0, tiled=True)

    grad_down, grad_up = pl.pallas_call(
        weight_gradient_kernel,
        out_shape=(shape((rank, width), f32), shape((rank, out_width), f32)),
        name="weight_gradient",
    )(recv_inputs, recv_grads, coef, down_factor)

    passed = pl.pallas_call(
        unplace_kernel,
        grid=(steps,),
        in_specs=[
            pl.BlockSpec((2 * tok_rows, slots), lambda c: (0, 0)),
            pl.BlockSpec((owners, group, block), lambda c: (0, 0, c)),
        ],
        out_specs=anywhere,
        out_shape=shape((tok_rows, width), bf16),
        scratch_shapes=[pltpu.VMEM((steps, 2 * tok_rows, block), bf16), pltpu.SemaphoreType.DMA((steps, 2))],
        name="unplace",
    )(back, returned)

    return (passed[None], grad_down.T[None, None], grad_up[None, None])


def solution(mesh):
    return jax.shard_map(
        local,
        mesh=mesh,
        in_specs=(
            P("segment", "owner", None),
            P("segment", "owner", None),
            P("owner", None),
            P(),
            P("segment", "owner", None, None),
            P("segment", "owner", None, None),
        ),
        out_specs=(
            P("segment", "owner", None),
            P("segment", "owner", None, None),
            P("segment", "owner", None, None),
        ),
        check_vma=False,
    )
```

```python
import jax
import jax.numpy as jnp
from jax import lax
from jax.experimental import pallas as pl
from jax.experimental.pallas import tpu as pltpu
from jax.sharding import PartitionSpec as P

adapter_scale = 2.0
row_limit = 4
group = 2 * row_limit
banks = 8
members = 8
bank_slots = 7
straight = 2
lines = 2 * bank_slots + 2
f32 = jnp.float32
bf16 = jnp.bfloat16


def dot(a, b, contract):
    return lax.dot_general(a, b, (contract, ((), ())), preferred_element_type=f32)


def iota(shape, axis):
    return lax.broadcasted_iota(jnp.int32, shape, axis)


def half_of(shape):
    return (iota(shape, 0) // row_limit) % 2


def place_gradient_kernel(tenant_ref, owner_ref, grad_ref, placing_ref, send_ref):
    tok_rows = tenant_ref.shape[1]
    owners = owner_ref.shape[1]
    slots = owners * group
    named = iota((owners, tok_rows), 0) == tenant_ref[...]
    before = (iota((tok_rows, tok_rows), 0) < iota((tok_rows, tok_rows), 1)).astype(bf16)
    rank = dot(named.astype(bf16), before, ((1,), (0,)))
    key = jnp.where(named, rank + 1.0, 0.0).astype(bf16)
    held = (iota((slots, owners), 0) // group == owner_ref[...]).astype(bf16)
    wide_key = dot(held, key, ((1,), (0,)))
    index = (iota((slots, tok_rows), 0) % row_limit + 1).astype(f32)
    placing = wide_key == index
    placing_ref[...] = placing.astype(bf16)
    half = half_of((slots, tok_rows))
    width = grad_ref.shape[1] // 2
    lower = jnp.where(placing & (half == 0), 1.0, 0.0).astype(bf16)
    upper = jnp.where(placing & (half == 1), 1.0, 0.0).astype(bf16)
    sent = dot(lower, grad_ref[:, :width], ((1,), (0,))) + dot(upper, grad_ref[:, width:], ((1,), (0,)))
    send_ref[...] = sent.astype(bf16).reshape(send_ref.shape)


def place_inputs_kernel(placing_ref, low_ref, high_ref, send_ref):
    placing = placing_ref[...]
    half = half_of(placing.shape)
    zero = jnp.zeros_like(placing)
    lower = jnp.where(half == 0, placing, zero)
    upper = jnp.where(half == 1, placing, zero)
    sent = dot(lower, low_ref[...], ((1,), (0,))) + dot(upper, high_ref[...], ((1,), (0,)))
    send_ref[...] = sent.astype(bf16).reshape(send_ref.shape)


def place_banks_kernel(tenant_ref, owner_ref, placing_ref, low_ref, high_ref, send_ref, back_ref, pick_ref, code_ref):
    tok_rows = tenant_ref.shape[1]
    owners = owner_ref.shape[1]
    total = banks * lines
    block = low_ref.shape[1]
    step = pl.program_id(0)

    @pl.when(step == 0)
    def _():
        placing = placing_ref[...].astype(f32)
        half = half_of(placing.shape)
        back_ref[:tok_rows] = jnp.where(half == 0, placing, 0.0).T.astype(bf16)
        back_ref[tok_rows:] = jnp.where(half == 1, placing, 0.0).T.astype(bf16)
        named = iota((owners, tok_rows), 0) == tenant_ref[...]
        named_bf16 = named.astype(bf16)
        before = (iota((tok_rows, tok_rows), 0) < iota((tok_rows, tok_rows), 1)).astype(bf16)
        rank = dot(named_bf16, before, ((1,), (0,)))
        late = (named & (rank >= straight)).astype(bf16)
        in_bank = dot((iota((banks, owners), 0) == owner_ref[...] // members).astype(bf16), late, ((1,), (0,)))
        bank_rank = dot(in_bank.astype(bf16), before, ((1,), (0,)))
        key = in_bank * (bank_rank + 1.0)
        most = jnp.max(key)
        slot = jnp.sum(key, axis=0, keepdims=True) - 1.0
        place = jnp.sum(jnp.where(named, rank, 0.0), axis=0, keepdims=True)
        member = jnp.broadcast_to((owner_ref[...] % members).astype(f32), (banks, owners)).astype(bf16)
        member = dot(member, named_bf16, ((1,), (0,)))
        code = in_bank * (member * straight + place - straight + 1.0)
        line = iota((tok_rows, tok_rows), 0)
        mine = ((line % bank_slots).astype(f32) == slot) & (line < 2 * bank_slots)
        codes = dot(code.astype(bf16), mine.astype(bf16), ((1,), (1,)))
        spread = (iota((total, banks), 0) // lines == iota((total, banks), 1)).astype(bf16)
        wide_key = dot(spread, key.astype(bf16), ((1,), (0,)))
        line = iota((total, tok_rows), 0) % lines
        pick = (wide_key == (line % bank_slots + 1).astype(f32)) & (line < 2 * bank_slots)
        pick_ref[0] = jnp.where(pick & (line < bank_slots), 1.0, 0.0).astype(bf16)
        pick_ref[1] = jnp.where(pick & (line >= bank_slots), 1.0, 0.0).astype(bf16)
        wide_code = dot(spread, codes.astype(bf16), ((1,), (0,)))
        code_ref[...] = jnp.where(line == lines - 2, wide_code, jnp.where(line == lines - 1, most, 0.0))

    sent = dot(pick_ref[0], low_ref[...], ((1,), (0,))) + dot(pick_ref[1], high_ref[...], ((1,), (0,)))
    send_ref[...] = sent.astype(bf16).reshape(send_ref.shape)

    @pl.when(step == 0)
    def _():
        first = sent[:, :tok_rows] + code_ref[...]
        send_ref[:, :, :tok_rows] = first.astype(bf16).reshape(banks, lines, tok_rows)


def place_straight_kernel(placing_ref, *refs):
    quarters, send_ref, pick_ref = refs[:4], refs[4], refs[5]

    @pl.when(pl.program_id(0) == 0)
    def _():
        placing = placing_ref[...].astype(f32).reshape(-1, group, placing_ref.shape[1])
        line = iota(placing.shape, 1)
        first = jnp.where(line % row_limit < straight, placing, pltpu.roll(placing, straight, 1))
        for q in range(4):
            pick_ref[q] = jnp.where(line // straight == q, first, 0.0).astype(bf16).reshape(placing_ref.shape)

    sent = dot(pick_ref[0], quarters[0][...], ((1,), (0,)))
    for q in range(1, 4):
        sent = sent + dot(pick_ref[q], quarters[q][...], ((1,), (0,)))
    send_ref[...] = sent.astype(bf16).reshape(send_ref.shape)


def route_kernel(member_ref, low_ref, high_ref, *refs):
    outs, pick_ref, most_ref = refs[:members], refs[members], refs[members + 1]
    block = low_ref.shape[2]
    rows = members * group

    @pl.when(pl.program_id(0) == 0)
    def _():
        x, core = member_ref[0] // 2, member_ref[0] % 2
        row, line = iota((rows, lines), 0), iota((rows, lines), 1)
        t = row // group
        to = (x + t // 2) % 4 * 2 + (core + t) % 2
        want = (to * straight + row % straight + 1).astype(f32)
        same_half = row % group // row_limit == line // bank_slots
        most = jnp.zeros((1, 128), f32)
        for y in range(banks):
            tail = low_ref[y, :, :128].astype(f32)
            codes = tail[lines - 2 : lines - 1, :lines]
            most = jnp.maximum(most, tail[lines - 1 :, :])
            pick_ref[y] = jnp.where((want == codes) & same_half, 1.0, 0.0).astype(bf16)
        most_ref[...] = jnp.broadcast_to(most, most_ref.shape)

    for y in range(banks):
        low = dot(pick_ref[y], low_ref[y], ((1,), (0,)))
        high = dot(pick_ref[y], high_ref[y], ((1,), (0,)))
        odd = iota(low.shape, 0) // straight % 2 == 1
        part = jnp.where(odd, high, low).astype(bf16).reshape(members, group, block)
        for t in range(members):
            outs[t][y] = part[t]
    most = jnp.broadcast_to(most_ref[:, :1], (group, block)).astype(bf16)
    for t in range(members):
        outs[t][banks] = most


def both_halves(x):
    blocks = x.reshape(x.shape[0] // group, group, x.shape[1])
    return (blocks + pltpu.roll(blocks, row_limit, 1)).reshape(x.shape)


def coef_kernel(grad_ref, up_ref, coef_ref, compact_ref):
    grads = grad_ref[...].reshape(coef_ref.shape[0], grad_ref.shape[2])
    width = grad_ref.shape[2]
    low = dot(grads, up_ref[:, :width], ((1,), (1,)))
    high = dot(grads, up_ref[:, width:], ((1,), (1,)))
    part = jnp.where(half_of(low.shape) == 0, low, high)
    coef = (adapter_scale * both_halves(part)).astype(bf16)
    coef_ref[...] = coef
    shape = (coef.shape[0], compact_ref.shape[1])
    row, column = iota(shape, 0), iota(shape, 1)
    first = row // group * group + row % row_limit == column // row_limit * group + column % row_limit
    picked = jnp.where(first & (half_of(shape) == 0), 1.0, 0.0).astype(bf16)
    compact_ref[...] = dot(coef, picked, ((0,), (0,))).astype(bf16)


def term_kernel(place_ref, coef_ref, low_ref, high_ref, out_ref, wide_ref):
    sections, rank, columns = coef_ref.shape

    @pl.when(pl.program_id(0) == 0)
    def _():
        place = place_ref[0]
        parts = []
        for k in range(sections):
            parts.append(jnp.where(place <= k, coef_ref[k], jnp.zeros_like(coef_ref[k])))
        shape = (columns, wide_ref.shape[0])
        column, row = iota(shape, 0), iota(shape, 1)
        same = column == row // group * row_limit + row % row_limit
        spread = jnp.where(same, 1.0, 0.0).astype(bf16)
        wide = dot(jnp.concatenate(parts, axis=0), spread, ((1,), (0,)))
        wide_ref[...] = wide.T.astype(bf16)

    coef = wide_ref[...]
    low = dot(coef, low_ref[...], ((1,), (0,)))
    high = dot(coef, high_ref[...], ((1,), (0,)))
    out = jnp.where(half_of(low.shape) == 0, low, high)
    out_ref[...] = out.astype(bf16).reshape(out_ref.shape)


def gradients(rows, grads, coef, down_ref, grad_down_ref, grad_up_ref):
    rank = coef.shape[1]
    width = rows.shape[1]
    out_width = grads.shape[1]
    half = half_of(coef.shape)
    zero = jnp.zeros_like(coef)
    pair = jnp.concatenate([jnp.where(half == 0, coef, zero), jnp.where(half == 1, coef, zero)], axis=1)
    down = dot(pair, rows, ((0,), (0,)))
    grad_down_ref[:, :width] = down[:rank]
    grad_down_ref[:, width:] = down[rank:]
    low = dot(rows, down_ref[:, :width], ((1,), (1,)))
    high = dot(rows, down_ref[:, width:], ((1,), (1,)))
    proj = both_halves(jnp.where(half == 0, low, high)).astype(bf16)
    pair = jnp.concatenate([jnp.where(half == 0, proj, zero), jnp.where(half == 1, proj, zero)], axis=1)
    up = dot(pair, grads, ((0,), (0,)))
    grad_up_ref[:, :out_width] = up[:rank]
    grad_up_ref[:, out_width:] = up[rank:]


def weight_gradient_kernel(rows_ref, grads_ref, coef_ref, down_ref, grad_down_ref, grad_up_ref):
    slots = coef_ref.shape[0]
    rows = rows_ref[...].reshape(slots, rows_ref.shape[2])
    grads = grads_ref[...].reshape(slots, grads_ref.shape[2])
    gradients(rows, grads, coef_ref[...], down_ref, grad_down_ref, grad_up_ref)


def add_gradients(rows, grads, coef, lines_of, down_ref, grad_down_ref, grad_up_ref):
    rank = coef.shape[1]
    width = rows.shape[1]
    out_width = grads.shape[1]
    line = iota(coef.shape, 0) % group
    zero = jnp.zeros_like(coef)
    parts = jnp.concatenate([jnp.where(line // straight == q, coef, zero) for q in range(4)], axis=1)
    down = dot(parts, rows, ((0,), (0,)))
    proj = jnp.zeros(coef.shape, f32)
    for q in range(4):
        here = slice(q * width, (q + 1) * width)
        grad_down_ref[:, here] += down[q * rank : (q + 1) * rank]
        proj = jnp.where(line // straight == q, dot(rows, down_ref[:, here], ((1,), (1,))), proj)
    proj = proj.reshape(-1, group, rank)
    proj = proj + pltpu.roll(proj, 4, 1)
    proj = (proj + pltpu.roll(proj, 2, 1)).reshape(coef.shape).astype(bf16)
    own = lines_of(line)
    half = line // row_limit
    pair = [jnp.where(own & (half == h), proj, zero) for h in range(2)]
    up = dot(jnp.concatenate(pair, axis=1), grads, ((0,), (0,)))
    grad_up_ref[:, :out_width] += up[:rank]
    grad_up_ref[:, out_width:] += up[rank:]


def bank_gradient_kernel(member_ref, rows_ref, grads_ref, coef_ref, down_ref, *refs):
    blocks, (grad_down_ref, grad_up_ref, most_ref) = refs[:members], refs[members:]
    rank = coef_ref.shape[3]
    out_width = grads_ref.shape[3]
    width = rows_ref.shape[2]
    slots = banks * members * group
    grad_down_ref[...] = jnp.zeros_like(grad_down_ref)
    grad_up_ref[...] = jnp.zeros_like(grad_up_ref)

    coef = coef_ref[...].reshape(banks * members, group, rank).astype(f32)
    first = iota(coef.shape, 1) % row_limit < straight
    coef = jnp.where(first, coef, pltpu.roll(coef, straight, 1)).reshape(slots, rank).astype(bf16)
    rows = rows_ref[...].reshape(slots, width)
    grads = grads_ref[...].reshape(slots, out_width)
    add_gradients(
        rows, grads, coef, lambda line: line % row_limit < straight, down_ref, grad_down_ref, grad_up_ref
    )

    x, core = member_ref[0] // 2, member_ref[0] % 2
    rows, coef, grads = [], [], []
    most = jnp.zeros((group, 128), f32)
    for t in range(members):
        source = (x + 4 - t // 2) % 4 * 2 + (core + t) % 2
        rows.append(blocks[t][:banks].reshape(banks * group, width))
        coef.append(coef_ref[:, pl.ds(source, 1)].reshape(banks, group, rank).astype(f32))
        grads.append(grads_ref[:, pl.ds(source, 1)].reshape(banks * group, out_width))
        most = jnp.maximum(most, blocks[t][banks, :, :128].astype(f32))
    most_ref[0] = jnp.max(most).astype(jnp.int32)
    rows, coef, grads = (jnp.concatenate(part, axis=0) for part in (rows, coef, grads))
    last = iota(coef.shape, 1) % row_limit >= straight
    coef = jnp.where(last, coef, pltpu.roll(coef, group - straight, 1)).reshape(slots, rank).astype(bf16)
    add_gradients(
        rows, grads, coef, lambda line: line % row_limit >= straight, down_ref, grad_down_ref, grad_up_ref
    )


def unplace_kernel(back_ref, rows_ref, out_ref):
    tok_rows = out_ref.shape[0]
    block = rows_ref.shape[2]
    rows = rows_ref[...].reshape(back_ref.shape[1], block)
    both = dot(back_ref[...], rows, ((1,), (0,))).astype(bf16)
    start = pl.multiple_of(pl.program_id(0) * block, block)
    out_ref[:, pl.ds(start, block)] = both[:tok_rows]
    start = pl.multiple_of(out_ref.shape[1] // 2 + pl.program_id(0) * block, block)
    out_ref[:, pl.ds(start, block)] = both[tok_rows:]


def local(
    layer_input_rows,
    output_gradient,
    tenant,
    adapter_owner_index,
    adapter_down_weight,
    adapter_up_weight,
):
    inputs = layer_input_rows[0]
    gradient_list = output_gradient[0]
    tok_rows, width = inputs.shape
    out_width = gradient_list.shape[1]
    owners = adapter_owner_index.shape[0]
    rank = adapter_up_weight.shape[2]
    slots = owners * group
    sections = lax.axis_size("segment")
    place = lax.axis_index("segment").astype(jnp.int32).reshape(1)
    down_factor = adapter_down_weight[0, 0].T
    up_factor = adapter_up_weight[0, 0]
    half_width = width // 2
    steps = 4
    block = half_width // steps
    shape = jax.ShapeDtypeStruct

    all_down = lax.all_gather(down_factor, "segment").reshape(sections * rank, width)

    owner_row = adapter_owner_index.reshape(1, owners)
    tenant_row = tenant.reshape(1, tok_rows)
    member = (lax.axis_index("owner") % members).astype(jnp.int32).reshape(1)

    placing, send_grads = pl.pallas_call(
        place_gradient_kernel,
        out_shape=(shape((slots, tok_rows), bf16), shape((owners, group, out_width // 2), bf16)),
        name="place_gradient",
    )(tenant_row, owner_row, gradient_list)
    recv_grads = lax.all_to_all(send_grads, "owner", split_axis=0, concat_axis=0, tiled=True)

    send_banks, back = pl.pallas_call(
        place_banks_kernel,
        grid=(steps,),
        in_specs=[
            pl.BlockSpec((1, tok_rows), lambda c: (0, 0)),
            pl.BlockSpec((1, owners), lambda c: (0, 0)),
            pl.BlockSpec((slots, tok_rows), lambda c: (0, 0)),
            pl.BlockSpec((tok_rows, block), lambda c: (0, c)),
            pl.BlockSpec((tok_rows, block), lambda c: (0, c + steps)),
        ],
        out_specs=(
            pl.BlockSpec((banks, lines, block), lambda c: (0, 0, c)),
            pl.BlockSpec((2 * tok_rows, slots), lambda c: (0, 0)),
        ),
        out_shape=(shape((banks, lines, half_width), bf16), shape((2 * tok_rows, slots), bf16)),
        scratch_shapes=[pltpu.VMEM((2, banks * lines, tok_rows), bf16), pltpu.VMEM((banks * lines, tok_rows), f32)],
        name="place_banks",
    )(tenant_row, owner_row, placing, inputs, inputs)

    coef, compact = pl.pallas_call(
        coef_kernel,
        out_shape=(shape((slots, rank), bf16), shape((rank, slots // 2), bf16)),
        name="coef",
    )(recv_grads, up_factor)

    same_member = [[y * members + m for y in range(banks)] for m in range(members)]
    recv_banks = lax.all_to_all(
        send_banks, "owner", split_axis=0, concat_axis=0, axis_index_groups=same_member, tiled=True
    )
    quarter = width // 4
    quarter_steps = 2
    quarter_block = quarter // quarter_steps
    send_straight = pl.pallas_call(
        place_straight_kernel,
        grid=(quarter_steps,),
        in_specs=[pl.BlockSpec((slots, tok_rows), lambda c: (0, 0))]
        + [
            pl.BlockSpec((tok_rows, quarter_block), lambda c, q=q: (0, q * quarter_steps + c)) for q in range(4)
        ],
        out_specs=pl.BlockSpec((owners, group, quarter_block), lambda c: (0, 0, c)),
        out_shape=shape((owners, group, quarter), bf16),
        scratch_shapes=[pltpu.VMEM((4, slots, tok_rows), bf16)],
        name="place_straight",
    )(placing, inputs, inputs, inputs, inputs)
    send_straight, recv_banks, compact = lax.optimization_barrier((send_straight, recv_banks, compact))
    recv_straight = lax.all_to_all(send_straight, "owner", split_axis=0, concat_axis=0, tiled=True)
    all_coef = lax.all_gather(compact, "segment")

    terms = pl.pallas_call(
        term_kernel,
        grid=(steps,),
        in_specs=[
            pl.BlockSpec(memory_space=pltpu.SMEM),
            pl.BlockSpec((sections, rank, slots // 2), lambda c: (0, 0, 0)),
            pl.BlockSpec((sections * rank, block), lambda c: (0, c)),
            pl.BlockSpec((sections * rank, block), lambda c: (0, c + steps)),
        ],
        out_specs=pl.BlockSpec((owners, group, block), lambda c: (0, 0, c)),
        out_shape=shape((owners, group, half_width), bf16),
        scratch_shapes=[pltpu.VMEM((slots, sections * rank), bf16)],
        name="term",
    )(place, all_coef, all_down, all_down)
    returned = lax.all_to_all(terms, "owner", split_axis=0, concat_axis=0, tiled=True)

    sent_blocks = pl.pallas_call(
        route_kernel,
        grid=(quarter_steps,),
        in_specs=[
            pl.BlockSpec(memory_space=pltpu.SMEM),
            pl.BlockSpec((banks, lines, quarter_block), lambda c: (0, 0, c)),
            pl.BlockSpec((banks, lines, quarter_block), lambda c: (0, 0, quarter_steps + c)),
        ],
        out_specs=[pl.BlockSpec((banks + 1, group, quarter_block), lambda c: (0, 0, c))] * members,
        out_shape=[shape((banks + 1, group, quarter), bf16)] * members,
        scratch_shapes=[pltpu.VMEM((banks, members * group, lines), bf16), pltpu.VMEM((group, 128), f32)],
        name="route",
    )(member, recv_banks, recv_banks)
    got_blocks = [sent_blocks[0]]
    for t in range(1, members):
        pairs = []
        for i in range(owners):
            y, x, core = i // members, i % members // 2, i % 2
            pairs.append((i, y * members + (x + t // 2) % 4 * 2 + (core + t) % 2))
        got_blocks.append(lax.ppermute(sent_blocks[t], "owner", pairs))

    smem = pl.BlockSpec(memory_space=pltpu.SMEM)
    vmem = pl.BlockSpec(memory_space=pltpu.VMEM)
    grad_down, grad_up, most = pl.pallas_call(
        bank_gradient_kernel,
        in_specs=[smem] + [vmem] * (4 + members),
        out_specs=(vmem, vmem, smem),
        out_shape=(shape((rank, width), f32), shape((rank, out_width), f32), shape((1,), jnp.int32)),
        name="bank_gradient",
    )(
        member,
        recv_straight,
        recv_grads.reshape(banks, members, group, out_width // 2),
        coef.reshape(banks, members, group, rank),
        down_factor,
        *got_blocks,
    )

    def direct(grad_down, grad_up, placing, inputs, recv_grads, coef, down_factor):
        send_inputs = pl.pallas_call(
            place_inputs_kernel,
            grid=(steps,),
            in_specs=[
                pl.BlockSpec((slots, tok_rows), lambda c: (0, 0)),
                pl.BlockSpec((tok_rows, block), lambda c: (0, c)),
                pl.BlockSpec((tok_rows, block), lambda c: (0, c + steps)),
            ],
            out_specs=pl.BlockSpec((owners, group, block), lambda c: (0, 0, c)),
            out_shape=shape((owners, group, half_width), bf16),
            name="place_inputs",
        )(placing, inputs, inputs)
        recv_inputs = lax.all_to_all(send_inputs, "owner", split_axis=0, concat_axis=0, tiled=True)
        return tuple(
            pl.pallas_call(
                weight_gradient_kernel,
                out_shape=(shape((rank, width), f32), shape((rank, out_width), f32)),
                name="weight_gradient",
            )(recv_inputs, recv_grads, coef, down_factor)
        )

    def kept(grad_down, grad_up, *rest):
        return grad_down, grad_up

    grad_down, grad_up, most, returned = lax.optimization_barrier((grad_down, grad_up, most, returned))
    grad_down, grad_up = lax.cond(
        most[0] > bank_slots, direct, kept, grad_down, grad_up, placing, inputs, recv_grads, coef, down_factor
    )

    passed = pl.pallas_call(
        unplace_kernel,
        grid=(steps,),
        in_specs=[
            pl.BlockSpec((2 * tok_rows, slots), lambda c: (0, 0)),
            pl.BlockSpec((owners, group, block), lambda c: (0, 0, c)),
        ],
        out_specs=pl.BlockSpec((tok_rows, width), lambda c: (0, 0)),
        out_shape=shape((tok_rows, width), bf16),
        name="unplace",
    )(back, returned)

    return (passed[None], grad_down.T[None, None], grad_up[None, None])


def solution(mesh):
    return jax.shard_map(
        local,
        mesh=mesh,
        in_specs=(
            P("segment", "owner", None),
            P("segment", "owner", None),
            P("owner", None),
            P(),
            P("segment", "owner", None, None),
            P("segment", "owner", None, None),
        ),
        out_specs=(
            P("segment", "owner", None),
            P("segment", "owner", None, None),
            P("segment", "owner", None, None),
        ),
        check_vma=False,
    )
```

```python
import jax
import jax.numpy as jnp
from jax import lax
from jax.experimental import pallas as pl
from jax.experimental.pallas import tpu as pltpu
from jax.sharding import PartitionSpec as P

adapter_scale = 2.0
row_limit = 4
group = 2 * row_limit
f32 = jnp.float32
bf16 = jnp.bfloat16


def dot(a, b, contract):
    return lax.dot_general(a, b, (contract, ((), ())), preferred_element_type=f32)


def iota(shape, axis):
    return lax.broadcasted_iota(jnp.int32, shape, axis)


def half_of(shape):
    return (iota(shape, 0) // row_limit) % 2


def place_gradient_kernel(tenant_ref, owner_ref, grad_ref, placing_ref, send_ref):
    tok_rows = tenant_ref.shape[1]
    owners = owner_ref.shape[1]
    slots = owners * group
    named = iota((owners, tok_rows), 0) == tenant_ref[...]
    before = (iota((tok_rows, tok_rows), 0) < iota((tok_rows, tok_rows), 1)).astype(bf16)
    rank = dot(named.astype(bf16), before, ((1,), (0,)))
    key = jnp.where(named, rank + 1.0, 0.0).astype(bf16)
    held = (iota((slots, owners), 0) // group == owner_ref[...]).astype(bf16)
    wide_key = dot(held, key, ((1,), (0,)))
    index = (iota((slots, tok_rows), 0) % row_limit + 1).astype(f32)
    placing = wide_key == index
    placing_ref[...] = placing.astype(bf16)
    half = half_of((slots, tok_rows))
    width = grad_ref.shape[1] // 2
    lower = jnp.where(placing & (half == 0), 1.0, 0.0).astype(bf16)
    upper = jnp.where(placing & (half == 1), 1.0, 0.0).astype(bf16)
    sent = dot(lower, grad_ref[:, :width], ((1,), (0,))) + dot(upper, grad_ref[:, width:], ((1,), (0,)))
    send_ref[...] = sent.astype(bf16).reshape(send_ref.shape)


def place_inputs_kernel(placing_ref, low_ref, high_ref, send_ref, back_ref):
    placing = placing_ref[...]
    half = half_of(placing.shape)
    zero = jnp.zeros_like(placing)
    lower = jnp.where(half == 0, placing, zero)
    upper = jnp.where(half == 1, placing, zero)

    @pl.when(pl.program_id(0) == 0)
    def _():
        back_ref[: lower.shape[1]] = lower.astype(f32).T.astype(bf16)
        back_ref[lower.shape[1] :] = upper.astype(f32).T.astype(bf16)

    sent = dot(lower, low_ref[...], ((1,), (0,))) + dot(upper, high_ref[...], ((1,), (0,)))
    send_ref[...] = sent.astype(bf16).reshape(send_ref.shape)


def both_halves(x):
    blocks = x.reshape(x.shape[0] // group, group, x.shape[1])
    return (blocks + pltpu.roll(blocks, row_limit, 1)).reshape(x.shape)


def coef_kernel(grad_ref, up_ref, coef_ref, compact_ref):
    grads = grad_ref[...].reshape(coef_ref.shape[0], grad_ref.shape[2])
    width = grad_ref.shape[2]
    low = dot(grads, up_ref[:, :width], ((1,), (1,)))
    high = dot(grads, up_ref[:, width:], ((1,), (1,)))
    part = jnp.where(half_of(low.shape) == 0, low, high)
    coef = both_halves(part).astype(bf16)
    coef_ref[...] = coef
    shape = (coef.shape[0], compact_ref.shape[1])
    row, column = iota(shape, 0), iota(shape, 1)
    first = row // group * group + row % row_limit == column // row_limit * group + column % row_limit
    picked = jnp.where(first & (half_of(shape) == 0), 1.0, 0.0).astype(bf16)
    compact_ref[...] = dot(coef, picked, ((0,), (0,))).astype(bf16)


def term_kernel(place_ref, coef_ref, low_ref, high_ref, out_ref, wide_ref):
    sections, rank, columns = coef_ref.shape

    @pl.when(pl.program_id(0) == 0)
    def _():
        place = place_ref[0]
        parts = []
        for k in range(sections):
            parts.append(jnp.where(place <= k, coef_ref[k], jnp.zeros_like(coef_ref[k])))
        shape = (columns, wide_ref.shape[0])
        column, row = iota(shape, 0), iota(shape, 1)
        same = column == row // group * row_limit + row % row_limit
        spread = jnp.where(same, 1.0, 0.0).astype(bf16)
        wide = dot(jnp.concatenate(parts, axis=0), spread, ((1,), (0,)))
        wide_ref[...] = wide.T.astype(bf16)

    coef = wide_ref[...]
    low = dot(coef, low_ref[...], ((1,), (0,)))
    high = dot(coef, high_ref[...], ((1,), (0,)))
    out = jnp.where(half_of(low.shape) == 0, low, high)
    out_ref[...] = out.astype(bf16).reshape(out_ref.shape)


def weight_gradient_kernel(rows_ref, grads_ref, coef_ref, down_ref, grad_down_ref, grad_up_ref):
    slots = coef_ref.shape[0]
    rank = coef_ref.shape[1]
    width = rows_ref.shape[2]
    out_width = grads_ref.shape[2]
    rows = rows_ref[...].reshape(slots, width)
    grads = grads_ref[...].reshape(slots, out_width)
    half = half_of((slots, rank))
    coef = coef_ref[...]
    zero = jnp.zeros_like(coef)
    pair = jnp.concatenate([jnp.where(half == 0, coef, zero), jnp.where(half == 1, coef, zero)], axis=1)
    down = dot(pair, rows, ((0,), (0,)))
    grad_down_ref[:, :width] = down[:rank]
    grad_down_ref[:, width:] = down[rank:]
    low = dot(rows, down_ref[:, :width], ((1,), (1,)))
    high = dot(rows, down_ref[:, width:], ((1,), (1,)))
    proj = both_halves(jnp.where(half == 0, low, high)).astype(bf16)
    pair = jnp.concatenate([jnp.where(half == 0, proj, zero), jnp.where(half == 1, proj, zero)], axis=1)
    up = dot(pair, grads, ((0,), (0,)))
    grad_up_ref[:, :out_width] = up[:rank]
    grad_up_ref[:, out_width:] = up[rank:]


def unplace_kernel(back_ref, rows_ref, out_ref):
    tok_rows = out_ref.shape[0]
    block = rows_ref.shape[2]
    rows = rows_ref[...].reshape(back_ref.shape[1], block)
    both = dot(back_ref[...], rows, ((1,), (0,))).astype(bf16)
    start = pl.multiple_of(pl.program_id(0) * block, block)
    out_ref[:, pl.ds(start, block)] = both[:tok_rows]
    start = pl.multiple_of(out_ref.shape[1] // 2 + pl.program_id(0) * block, block)
    out_ref[:, pl.ds(start, block)] = both[tok_rows:]


def local(
    layer_input_rows,
    output_gradient,
    tenant,
    adapter_owner_index,
    adapter_down_weight,
    adapter_up_weight,
):
    inputs = layer_input_rows[0]
    gradient_list = output_gradient[0]
    tok_rows, width = inputs.shape
    out_width = gradient_list.shape[1]
    owners = adapter_owner_index.shape[0]
    rank = adapter_up_weight.shape[2]
    slots = owners * group
    sections = lax.axis_size("segment")
    place = lax.axis_index("segment").astype(jnp.int32).reshape(1)
    down_factor = adapter_down_weight[0, 0].T
    up_factor = adapter_up_weight[0, 0]
    half_width = width // 2
    steps = 4
    block = half_width // steps
    shape = jax.ShapeDtypeStruct

    all_down = lax.all_gather(down_factor, "segment").reshape(sections * rank, width)

    placing, send_grads = pl.pallas_call(
        place_gradient_kernel,
        out_shape=(shape((slots, tok_rows), bf16), shape((owners, group, out_width // 2), bf16)),
        name="place_gradient",
    )(tenant.reshape(1, tok_rows), adapter_owner_index.reshape(1, owners), gradient_list)
    recv_grads = lax.all_to_all(send_grads, "owner", split_axis=0, concat_axis=0, tiled=True)

    send_inputs, back = pl.pallas_call(
        place_inputs_kernel,
        grid=(steps,),
        in_specs=[
            pl.BlockSpec((slots, tok_rows), lambda c: (0, 0)),
            pl.BlockSpec((tok_rows, block), lambda c: (0, c)),
            pl.BlockSpec((tok_rows, block), lambda c: (0, c + steps)),
        ],
        out_specs=(
            pl.BlockSpec((owners, group, block), lambda c: (0, 0, c)),
            pl.BlockSpec((2 * tok_rows, slots), lambda c: (0, 0)),
        ),
        out_shape=(shape((owners, group, half_width), bf16), shape((2 * tok_rows, slots), bf16)),
        name="place_inputs",
    )(placing, inputs, inputs)

    coef, compact = pl.pallas_call(
        coef_kernel,
        out_shape=(shape((slots, rank), bf16), shape((rank, slots // 2), bf16)),
        name="coef",
    )(recv_grads * jnp.asarray(adapter_scale, bf16), up_factor)

    recv_inputs = lax.all_to_all(send_inputs, "owner", split_axis=0, concat_axis=0, tiled=True)
    all_coef = lax.all_gather(compact, "segment")

    terms = pl.pallas_call(
        term_kernel,
        grid=(steps,),
        in_specs=[
            pl.BlockSpec(memory_space=pltpu.SMEM),
            pl.BlockSpec((sections, rank, slots // 2), lambda c: (0, 0, 0)),
            pl.BlockSpec((sections * rank, block), lambda c: (0, c)),
            pl.BlockSpec((sections * rank, block), lambda c: (0, c + steps)),
        ],
        out_specs=pl.BlockSpec((owners, group, block), lambda c: (0, 0, c)),
        out_shape=shape((owners, group, half_width), bf16),
        scratch_shapes=[pltpu.VMEM((slots, sections * rank), bf16)],
        name="term",
    )(place, all_coef, all_down, all_down)
    returned = lax.all_to_all(terms, "owner", split_axis=0, concat_axis=0, tiled=True)

    grad_down, grad_up = pl.pallas_call(
        weight_gradient_kernel,
        out_shape=(shape((rank, width), f32), shape((rank, out_width), f32)),
        name="weight_gradient",
    )(recv_inputs, recv_grads, coef, down_factor)

    passed = pl.pallas_call(
        unplace_kernel,
        grid=(steps,),
        in_specs=[
            pl.BlockSpec((2 * tok_rows, slots), lambda c: (0, 0)),
            pl.BlockSpec((owners, group, block), lambda c: (0, 0, c)),
        ],
        out_specs=pl.BlockSpec((tok_rows, width), lambda c: (0, 0)),
        out_shape=shape((tok_rows, width), bf16),
        name="unplace",
    )(back, returned)

    return (passed[None], grad_down.T[None, None], grad_up[None, None])


def solution(mesh):
    return jax.shard_map(
        local,
        mesh=mesh,
        in_specs=(
            P("segment", "owner", None),
            P("segment", "owner", None),
            P("owner", None),
            P(),
            P("segment", "owner", None, None),
            P("segment", "owner", None, None),
        ),
        out_specs=(
            P("segment", "owner", None),
            P("segment", "owner", None, None),
            P("segment", "owner", None, None),
        ),
        check_vma=False,
    )
```

```python
import jax
import jax.numpy as jnp
from jax import lax
from jax.experimental import pallas as pl
from jax.experimental.pallas import tpu as pltpu
from jax.sharding import PartitionSpec as P

adapter_scale = 2.0
row_limit = 4
group = 2 * row_limit
f32 = jnp.float32
bf16 = jnp.bfloat16


def dot(a, b, contract):
    return lax.dot_general(a, b, (contract, ((), ())), preferred_element_type=f32)


def iota(shape, axis):
    return lax.broadcasted_iota(jnp.int32, shape, axis)


def half_of(shape):
    return (iota(shape, 0) // row_limit) % 2


def place_gradient_kernel(tenant_ref, owner_ref, grad_ref, placing_ref, send_ref):
    tok_rows = tenant_ref.shape[1]
    owners = owner_ref.shape[1]
    width = grad_ref.shape[1] // 2
    named = iota((owners, tok_rows), 0) == tenant_ref[...]
    before = (iota((tok_rows, tok_rows), 0) < iota((tok_rows, tok_rows), 1)).astype(bf16)
    rank = dot(named.astype(bf16), before, ((1,), (0,)))
    key = jnp.where(named, rank + 1.0, 0.0).astype(bf16)
    held = (iota((owners, owners), 0) == owner_ref[...]).astype(bf16)
    key = dot(held, key, ((1,), (0,)))
    blocks = (owners, group, tok_rows)
    line = iota(blocks, 1)
    placing = jnp.broadcast_to(key[:, None, :], blocks) == (line % row_limit + 1).astype(f32)
    rows = (owners * group, tok_rows)
    placing_ref[...] = jnp.where(placing, 1.0, 0.0).reshape(rows).astype(bf16)
    lower = jnp.where(placing & (line < row_limit), 1.0, 0.0).reshape(rows).astype(bf16)
    upper = jnp.where(placing & (line >= row_limit), 1.0, 0.0).reshape(rows).astype(bf16)
    grads = jnp.concatenate([grad_ref[:, :width], grad_ref[:, width:]], axis=0)
    sent = dot(jnp.concatenate([lower, upper], axis=1), grads, ((1,), (0,)))
    send_ref[...] = sent.astype(bf16).reshape(send_ref.shape)


def place_inputs_kernel(placing_ref, low_ref, high_ref, send_ref, back_ref):
    placing = placing_ref[...]
    half = half_of(placing.shape)
    zero = jnp.zeros_like(placing)
    lower = jnp.where(half == 0, placing, zero)
    upper = jnp.where(half == 1, placing, zero)

    @pl.when(pl.program_id(0) == 0)
    def _():
        back_ref[: lower.shape[1]] = lower.astype(f32).T.astype(bf16)
        back_ref[lower.shape[1] :] = upper.astype(f32).T.astype(bf16)

    sent = dot(lower, low_ref[...], ((1,), (0,))) + dot(upper, high_ref[...], ((1,), (0,)))
    send_ref[...] = sent.astype(bf16).reshape(send_ref.shape)


def both_halves(x):
    blocks = x.reshape(x.shape[0] // group, group, x.shape[1])
    return (blocks + pltpu.roll(blocks, row_limit, 1)).reshape(x.shape)


def coef_kernel(grad_ref, up_ref, coef_ref, compact_ref):
    grads = grad_ref[...].reshape(coef_ref.shape[0], grad_ref.shape[2])
    width = grad_ref.shape[2]
    low = dot(grads, up_ref[:, :width], ((1,), (1,)))
    high = dot(grads, up_ref[:, width:], ((1,), (1,)))
    part = jnp.where(half_of(low.shape) == 0, low, high)
    coef = (adapter_scale * both_halves(part)).astype(bf16)
    coef_ref[...] = coef
    shape = (coef.shape[0], compact_ref.shape[1])
    row, column = iota(shape, 0), iota(shape, 1)
    first = row // group * group + row % row_limit == column // row_limit * group + column % row_limit
    picked = jnp.where(first & (half_of(shape) == 0), 1.0, 0.0).astype(bf16)
    compact_ref[...] = dot(coef, picked, ((0,), (0,))).astype(bf16)


def term_kernel(place_ref, coef_ref, low_ref, high_ref, out_ref, wide_ref):
    sections, rank, columns = coef_ref.shape

    @pl.when(pl.program_id(0) == 0)
    def _():
        place = place_ref[0]
        parts = []
        for k in range(sections):
            parts.append(jnp.where(place <= k, coef_ref[k], jnp.zeros_like(coef_ref[k])))
        shape = (columns, wide_ref.shape[0])
        column, row = iota(shape, 0), iota(shape, 1)
        same = column == row // group * row_limit + row % row_limit
        spread = jnp.where(same, 1.0, 0.0).astype(bf16)
        wide = dot(jnp.concatenate(parts, axis=0), spread, ((1,), (0,)))
        wide_ref[...] = wide.T.astype(bf16)

    coef = wide_ref[...]
    low = dot(coef, low_ref[...], ((1,), (0,)))
    high = dot(coef, high_ref[...], ((1,), (0,)))
    out = jnp.where(half_of(low.shape) == 0, low, high)
    out_ref[...] = out.astype(bf16).reshape(out_ref.shape)


def weight_gradient_kernel(rows_ref, grads_ref, coef_ref, down_ref, grad_down_ref, grad_up_ref):
    slots = coef_ref.shape[0]
    rank = coef_ref.shape[1]
    width = rows_ref.shape[2]
    out_width = grads_ref.shape[2]
    rows = rows_ref[...].reshape(slots, width)
    grads = grads_ref[...].reshape(slots, out_width)
    half = half_of((slots, rank))
    coef = coef_ref[...]
    zero = jnp.zeros_like(coef)
    pair = jnp.concatenate([jnp.where(half == 0, coef, zero), jnp.where(half == 1, coef, zero)], axis=1)
    down = dot(pair, rows, ((0,), (0,)))
    grad_down_ref[:, :width] = down[:rank]
    grad_down_ref[:, width:] = down[rank:]
    low = dot(rows, down_ref[:, :width], ((1,), (1,)))
    high = dot(rows, down_ref[:, width:], ((1,), (1,)))
    proj = both_halves(jnp.where(half == 0, low, high)).astype(bf16)
    pair = jnp.concatenate([jnp.where(half == 0, proj, zero), jnp.where(half == 1, proj, zero)], axis=1)
    up = dot(pair, grads, ((0,), (0,)))
    grad_up_ref[:, :out_width] = up[:rank]
    grad_up_ref[:, out_width:] = up[rank:]


def unplace_kernel(back_ref, rows_ref, out_hbm, out_ref, sems):
    steps = out_ref.shape[0]
    tok_rows = out_hbm.shape[0]
    block = rows_ref.shape[2]
    step = pl.program_id(0)

    def write(c, h):
        start = pl.multiple_of((h * steps + c) * block, block)
        here = out_hbm.at[:, pl.ds(start, block)]
        return pltpu.make_async_copy(out_ref.at[c, pl.ds(h * tok_rows, tok_rows)], here, sems.at[c, h])

    rows = rows_ref[...].reshape(back_ref.shape[1], block)
    out_ref[step] = dot(back_ref[...], rows, ((1,), (0,))).astype(bf16)
    write(step, 0).start()
    write(step, 1).start()

    @pl.when(step == steps - 1)
    def _():
        for c in range(steps):
            write(c, 0).wait()
            write(c, 1).wait()


def exchange(blocks):
    return lax.all_to_all(blocks, "owner", split_axis=0, concat_axis=0, tiled=True)


def local(
    layer_input_rows,
    output_gradient,
    tenant,
    adapter_owner_index,
    adapter_down_weight,
    adapter_up_weight,
):
    inputs = layer_input_rows[0]
    gradient_list = output_gradient[0]
    tok_rows, width = inputs.shape
    out_width = gradient_list.shape[1]
    owners = adapter_owner_index.shape[0]
    rank = adapter_up_weight.shape[2]
    slots = owners * group
    sections = lax.axis_size("segment")
    place = lax.axis_index("segment").astype(jnp.int32).reshape(1)
    down_factor = adapter_down_weight[0, 0].T
    up_factor = adapter_up_weight[0, 0]
    half_width = width // 2
    steps = 4
    block = half_width // steps
    shape = jax.ShapeDtypeStruct
    vmem = pl.BlockSpec(memory_space=pltpu.VMEM)

    all_down = lax.all_gather(down_factor, "segment").reshape(sections * rank, width)

    placing, send_grads = pl.pallas_call(
        place_gradient_kernel,
        out_shape=(shape((slots, tok_rows), bf16), shape((owners, group, out_width // 2), bf16)),
        name="place_gradient",
    )(tenant.reshape(1, tok_rows), adapter_owner_index.reshape(1, owners), gradient_list)
    recv_grads = pltpu.with_memory_space_constraint(exchange(send_grads), pltpu.VMEM)

    send_inputs, back = pl.pallas_call(
        place_inputs_kernel,
        grid=(steps,),
        in_specs=[
            pl.BlockSpec((slots, tok_rows), lambda c: (0, 0)),
            pl.BlockSpec((tok_rows, block), lambda c: (0, c)),
            pl.BlockSpec((tok_rows, block), lambda c: (0, c + steps)),
        ],
        out_specs=(
            pl.BlockSpec((owners, group, block), lambda c: (0, 0, c)),
            pl.BlockSpec((2 * tok_rows, slots), lambda c: (0, 0)),
        ),
        out_shape=(shape((owners, group, half_width), bf16), shape((2 * tok_rows, slots), bf16)),
        name="place_inputs",
    )(placing, inputs, inputs)

    coef, compact = pl.pallas_call(
        coef_kernel,
        in_specs=[vmem, vmem],
        out_shape=(shape((slots, rank), bf16), shape((rank, slots // 2), bf16)),
        name="coef",
    )(recv_grads, up_factor)

    recv_inputs = pltpu.with_memory_space_constraint(exchange(send_inputs), pltpu.VMEM)
    all_coef = lax.all_gather(compact, "segment")

    terms = pl.pallas_call(
        term_kernel,
        grid=(steps,),
        in_specs=[
            pl.BlockSpec(memory_space=pltpu.SMEM),
            pl.BlockSpec((sections, rank, slots // 2), lambda c: (0, 0, 0)),
            pl.BlockSpec((sections * rank, block), lambda c: (0, c)),
            pl.BlockSpec((sections * rank, block), lambda c: (0, c + steps)),
        ],
        out_specs=pl.BlockSpec((owners, group, block), lambda c: (0, 0, c)),
        out_shape=shape((owners, group, half_width), bf16),
        scratch_shapes=[pltpu.VMEM((slots, sections * rank), bf16)],
        name="term",
    )(place, all_coef, all_down, all_down)
    returned = exchange(terms)

    grad_down, grad_up = pl.pallas_call(
        weight_gradient_kernel,
        in_specs=[vmem, vmem, vmem, vmem],
        out_shape=(shape((rank, width), f32), shape((rank, out_width), f32)),
        name="weight_gradient",
    )(recv_inputs, recv_grads, coef, down_factor)

    back_steps = 2
    back_block = half_width // back_steps
    passed = pl.pallas_call(
        unplace_kernel,
        grid=(back_steps,),
        in_specs=[
            pl.BlockSpec((2 * tok_rows, slots), lambda c: (0, 0)),
            pl.BlockSpec((owners, group, back_block), lambda c: (0, 0, c)),
        ],
        out_specs=pl.BlockSpec(memory_space=pl.ANY),
        out_shape=shape((tok_rows, width), bf16),
        scratch_shapes=[
            pltpu.VMEM((back_steps, 2 * tok_rows, back_block), bf16),
            pltpu.SemaphoreType.DMA((back_steps, 2)),
        ],
        name="unplace",
    )(back, returned)

    return (passed[None], grad_down.T[None, None], grad_up[None, None])


def solution(mesh):
    return jax.shard_map(
        local,
        mesh=mesh,
        in_specs=(
            P("segment", "owner", None),
            P("segment", "owner", None),
            P("owner", None),
            P(),
            P("segment", "owner", None, None),
            P("segment", "owner", None, None),
        ),
        out_specs=(
            P("segment", "owner", None),
            P("segment", "owner", None, None),
            P("segment", "owner", None, None),
        ),
        check_vma=False,
    )
```

```python
import jax
import jax.numpy as jnp
from jax import lax
from jax.experimental import pallas as pl
from jax.experimental.pallas import tpu as pltpu
from jax.sharding import PartitionSpec as P

adapter_scale = 2.0
row_limit = 4
group = 2 * row_limit
f32 = jnp.float32
bf16 = jnp.bfloat16


def dot(a, b, contract):
    return lax.dot_general(a, b, (contract, ((), ())), preferred_element_type=f32)


def iota(shape, axis):
    return lax.broadcasted_iota(jnp.int32, shape, axis)


def half_of(shape):
    return (iota(shape, 0) // row_limit) % 2


def place_gradient_kernel(tenant_ref, owner_ref, grad_ref, placing_ref, send_ref):
    tok_rows = tenant_ref.shape[1]
    owners = owner_ref.shape[1]
    width = grad_ref.shape[1] // 2
    named = iota((owners, tok_rows), 0) == tenant_ref[...]
    before = (iota((tok_rows, tok_rows), 0) < iota((tok_rows, tok_rows), 1)).astype(bf16)
    rank = dot(named.astype(bf16), before, ((1,), (0,)))
    key = jnp.where(named, rank + 1.0, 0.0).astype(bf16)
    held = (iota((owners, owners), 0) == owner_ref[...]).astype(bf16)
    key = dot(held, key, ((1,), (0,)))
    blocks = (owners, group, tok_rows)
    line = iota(blocks, 1)
    placing = jnp.broadcast_to(key[:, None, :], blocks) == (line % row_limit + 1).astype(f32)
    rows = (owners * group, tok_rows)
    placing_ref[...] = jnp.where(placing, 1.0, 0.0).reshape(rows).astype(bf16)
    lower = jnp.where(placing & (line < row_limit), 1.0, 0.0).reshape(rows).astype(bf16)
    upper = jnp.where(placing & (line >= row_limit), 1.0, 0.0).reshape(rows).astype(bf16)
    grads = jnp.concatenate([grad_ref[:, :width], grad_ref[:, width:]], axis=0)
    sent = dot(jnp.concatenate([lower, upper], axis=1), grads, ((1,), (0,)))
    send_ref[...] = sent.astype(bf16).reshape(send_ref.shape)


def place_inputs_kernel(placing_ref, low_ref, high_ref, send_ref, back_ref):
    placing = placing_ref[...]
    half = half_of(placing.shape)
    zero = jnp.zeros_like(placing)
    lower = jnp.where(half == 0, placing, zero)
    upper = jnp.where(half == 1, placing, zero)

    @pl.when(pl.program_id(0) == 0)
    def _():
        back_ref[: lower.shape[1]] = lower.astype(f32).T.astype(bf16)
        back_ref[lower.shape[1] :] = upper.astype(f32).T.astype(bf16)

    sent = dot(lower, low_ref[...], ((1,), (0,))) + dot(upper, high_ref[...], ((1,), (0,)))
    send_ref[...] = sent.astype(bf16).reshape(send_ref.shape)


def both_halves(x):
    blocks = x.reshape(x.shape[0] // group, group, x.shape[1])
    return (blocks + pltpu.roll(blocks, row_limit, 1)).reshape(x.shape)


def coef_kernel(grad_ref, up_ref, coef_ref, compact_ref):
    grads = grad_ref[...].reshape(coef_ref.shape[0], grad_ref.shape[2])
    width = grad_ref.shape[2]
    low = dot(grads, up_ref[:, :width], ((1,), (1,)))
    high = dot(grads, up_ref[:, width:], ((1,), (1,)))
    part = jnp.where(half_of(low.shape) == 0, low, high)
    exact = adapter_scale * both_halves(part)
    coef = exact.astype(bf16)
    rest = (exact - coef.astype(f32)).astype(bf16)
    coef_ref[...] = coef
    shape = (coef.shape[0], compact_ref.shape[1])
    row, column = iota(shape, 0), iota(shape, 1)
    first = row // group * group + row % row_limit == column // row_limit * group + column % row_limit
    picked = jnp.where(first & (half_of(shape) == 0), 1.0, 0.0).astype(bf16)
    compact_ref[...] = dot(jnp.concatenate([coef, rest], axis=1), picked, ((0,), (0,))).astype(bf16)


def term_kernel(place_ref, coef_ref, low_ref, high_ref, out_ref, wide_ref):
    sections, rank, columns = coef_ref.shape
    rank = rank // 2

    @pl.when(pl.program_id(0) == 0)
    def _():
        place = place_ref[0]
        parts = []
        for k in range(sections):
            parts.append(jnp.where(place <= k, coef_ref[k], jnp.zeros_like(coef_ref[k])))
        shape = (columns, wide_ref.shape[1])
        column, row = iota(shape, 0), iota(shape, 1)
        same = column == row // group * row_limit + row % row_limit
        spread = jnp.where(same, 1.0, 0.0).astype(bf16)
        for level in range(2):
            here = slice(level * rank, (level + 1) * rank)
            wide = dot(jnp.concatenate([part[here] for part in parts], axis=0), spread, ((1,), (0,)))
            wide_ref[level] = wide.T.astype(bf16)

    coef, rest = wide_ref[0], wide_ref[1]
    low = dot(coef, low_ref[...], ((1,), (0,))) + dot(rest, low_ref[...], ((1,), (0,)))
    high = dot(coef, high_ref[...], ((1,), (0,))) + dot(rest, high_ref[...], ((1,), (0,)))
    out = jnp.where(half_of(low.shape) == 0, low, high)
    out_ref[...] = out.astype(bf16).reshape(out_ref.shape)


def weight_gradient_kernel(rows_ref, grads_ref, coef_ref, down_ref, grad_down_ref, grad_up_ref):
    slots = coef_ref.shape[0]
    rank = coef_ref.shape[1]
    width = rows_ref.shape[2]
    out_width = grads_ref.shape[2]
    rows = rows_ref[...].reshape(slots, width)
    grads = grads_ref[...].reshape(slots, out_width)
    half = half_of((slots, rank))
    coef = coef_ref[...]
    zero = jnp.zeros_like(coef)
    pair = jnp.concatenate([jnp.where(half == 0, coef, zero), jnp.where(half == 1, coef, zero)], axis=1)
    down = dot(pair, rows, ((0,), (0,)))
    grad_down_ref[:, :width] = down[:rank]
    grad_down_ref[:, width:] = down[rank:]
    low = dot(rows, down_ref[:, :width], ((1,), (1,)))
    high = dot(rows, down_ref[:, width:], ((1,), (1,)))
    proj = both_halves(jnp.where(half == 0, low, high)).astype(bf16)
    pair = jnp.concatenate([jnp.where(half == 0, proj, zero), jnp.where(half == 1, proj, zero)], axis=1)
    up = dot(pair, grads, ((0,), (0,)))
    grad_up_ref[:, :out_width] = up[:rank]
    grad_up_ref[:, out_width:] = up[rank:]


def unplace_kernel(back_ref, rows_ref, out_hbm, out_ref, sems):
    steps = out_ref.shape[0]
    tok_rows = out_hbm.shape[0]
    block = rows_ref.shape[2]
    step = pl.program_id(0)

    def write(c, h):
        start = pl.multiple_of((h * steps + c) * block, block)
        here = out_hbm.at[:, pl.ds(start, block)]
        return pltpu.make_async_copy(out_ref.at[c, pl.ds(h * tok_rows, tok_rows)], here, sems.at[c, h])

    rows = rows_ref[...].reshape(back_ref.shape[1], block)
    out_ref[step] = dot(back_ref[...], rows, ((1,), (0,))).astype(bf16)
    write(step, 0).start()
    write(step, 1).start()

    @pl.when(step == steps - 1)
    def _():
        for c in range(steps):
            write(c, 0).wait()
            write(c, 1).wait()


def exchange(blocks):
    return lax.all_to_all(blocks, "owner", split_axis=0, concat_axis=0, tiled=True)


def local(
    layer_input_rows,
    output_gradient,
    tenant,
    adapter_owner_index,
    adapter_down_weight,
    adapter_up_weight,
):
    inputs = layer_input_rows[0]
    gradient_list = output_gradient[0]
    tok_rows, width = inputs.shape
    out_width = gradient_list.shape[1]
    owners = adapter_owner_index.shape[0]
    rank = adapter_up_weight.shape[2]
    slots = owners * group
    sections = lax.axis_size("segment")
    place = lax.axis_index("segment").astype(jnp.int32).reshape(1)
    down_factor = adapter_down_weight[0, 0].T
    up_factor = adapter_up_weight[0, 0]
    half_width = width // 2
    steps = 4
    block = half_width // steps
    shape = jax.ShapeDtypeStruct
    vmem = pl.BlockSpec(memory_space=pltpu.VMEM)

    all_down = lax.all_gather(down_factor, "segment").reshape(sections * rank, width)

    placing, send_grads = pl.pallas_call(
        place_gradient_kernel,
        out_shape=(shape((slots, tok_rows), bf16), shape((owners, group, out_width // 2), bf16)),
        name="place_gradient",
    )(tenant.reshape(1, tok_rows), adapter_owner_index.reshape(1, owners), gradient_list)
    recv_grads = pltpu.with_memory_space_constraint(exchange(send_grads), pltpu.VMEM)

    send_inputs, back = pl.pallas_call(
        place_inputs_kernel,
        grid=(steps,),
        in_specs=[
            pl.BlockSpec((slots, tok_rows), lambda c: (0, 0)),
            pl.BlockSpec((tok_rows, block), lambda c: (0, c)),
            pl.BlockSpec((tok_rows, block), lambda c: (0, c + steps)),
        ],
        out_specs=(
            pl.BlockSpec((owners, group, block), lambda c: (0, 0, c)),
            pl.BlockSpec((2 * tok_rows, slots), lambda c: (0, 0)),
        ),
        out_shape=(shape((owners, group, half_width), bf16), shape((2 * tok_rows, slots), bf16)),
        name="place_inputs",
    )(placing, inputs, inputs)

    coef, compact = pl.pallas_call(
        coef_kernel,
        in_specs=[vmem, vmem],
        out_shape=(shape((slots, rank), bf16), shape((2 * rank, slots // 2), bf16)),
        name="coef",
    )(recv_grads, up_factor)

    recv_inputs = pltpu.with_memory_space_constraint(exchange(send_inputs), pltpu.VMEM)
    all_coef = lax.all_gather(compact, "segment")

    terms = pl.pallas_call(
        term_kernel,
        grid=(steps,),
        in_specs=[
            pl.BlockSpec(memory_space=pltpu.SMEM),
            pl.BlockSpec((sections, 2 * rank, slots // 2), lambda c: (0, 0, 0)),
            pl.BlockSpec((sections * rank, block), lambda c: (0, c)),
            pl.BlockSpec((sections * rank, block), lambda c: (0, c + steps)),
        ],
        out_specs=pl.BlockSpec((owners, group, block), lambda c: (0, 0, c)),
        out_shape=shape((owners, group, half_width), bf16),
        scratch_shapes=[pltpu.VMEM((2, slots, sections * rank), bf16)],
        name="term",
    )(place, all_coef, all_down, all_down)
    returned = exchange(terms)

    grad_down, grad_up = pl.pallas_call(
        weight_gradient_kernel,
        in_specs=[vmem, vmem, vmem, vmem],
        out_shape=(shape((rank, width), f32), shape((rank, out_width), f32)),
        name="weight_gradient",
    )(recv_inputs, recv_grads, coef, down_factor)

    back_steps = 2
    back_block = half_width // back_steps
    passed = pl.pallas_call(
        unplace_kernel,
        grid=(back_steps,),
        in_specs=[
            pl.BlockSpec((2 * tok_rows, slots), lambda c: (0, 0)),
            pl.BlockSpec((owners, group, back_block), lambda c: (0, 0, c)),
        ],
        out_specs=pl.BlockSpec(memory_space=pl.ANY),
        out_shape=shape((tok_rows, width), bf16),
        scratch_shapes=[
            pltpu.VMEM((back_steps, 2 * tok_rows, back_block), bf16),
            pltpu.SemaphoreType.DMA((back_steps, 2)),
        ],
        name="unplace",
    )(back, returned)

    return (passed[None], grad_down.T[None, None], grad_up[None, None])


def solution(mesh):
    return jax.shard_map(
        local,
        mesh=mesh,
        in_specs=(
            P("segment", "owner", None),
            P("segment", "owner", None),
            P("owner", None),
            P(),
            P("segment", "owner", None, None),
            P("segment", "owner", None, None),
        ),
        out_specs=(
            P("segment", "owner", None),
            P("segment", "owner", None, None),
            P("segment", "owner", None, None),
        ),
        check_vma=False,
    )
```
